32 devices in a mesh: block: 16 (over z, x, core), lane: 2 (over y).
Axes of the slice: x: 2, y: 2, z: 4, core: 2. Of those that a mesh axis runs over, the one named last changes fastest.
Arguments:
- images: float32 [8192, 1152], P('block'), may hold values from -1.253025 to 1.253025
- texts: float32 [8192, 1152], P('block'), may hold values from -1.253025 to 1.253025
- labels: int32 [8192], P('block'), may hold values from 0 to 8191, each once
Outputs:
- image_grad: float32 [8192, 1152], P(('block', 'lane'))
- text_grad: float32 [8192, 1152], P(('block', 'lane'))
The draws below stay inside these ranges and needn't reach their ends.
Inputs may be any that keep to these rules, and one draw needn't show every extreme that they name: `labels`: each text row is the partner of exactly one image row.
All inputs are finite; a program needn't handle non-finite values.
Results may differ from the reference program's by a relative error of at most 0.004.
Values may be sent and summed in bfloat16 or wider, within the bound.
A program may use at most 64 MiB of HBM per device.

```python
import jax
import jax.numpy as jnp
from jax import lax

D = 1152
ROWS_DEV = 512
TOTAL = 8192


def block_levels(key, extent, pieces, least, largest):
    def one(axis_at, parts):
        draws = jax.random.uniform(jax.random.fold_in(jax.random.fold_in(key, 6), axis_at), (parts,), jnp.float32, least / len(pieces), largest / len(pieces))
        return jnp.repeat(jnp.exp(draws), extent[axis_at] // parts).reshape((-1,) + (1,) * (len(extent) - axis_at - 1))

    level = one(*pieces[0])
    for cut in pieces[1:]:
        level = level * one(*cut)
    return level


def normal_values(own_key, shape, scale, bound, pieces=(), held_as=jnp.bfloat16):
    array = jax.random.normal(own_key, shape, jnp.float32) * scale
    if len(pieces) > 0:
        array = block_levels(own_key, shape, pieces, -0.22, 0.18) * array
    return jnp.clip(array, min=-bound, max=bound).astype(held_as)


def setup_inputs(seed: int = 0) -> dict:
    splits = jax.random.split(jax.random.key(seed), 4)
    images = normal_values(splits[0], (TOTAL, D), (1.22 * D ** -0.25), 1.253025, ((0, 16),), jnp.float32)
    texts = normal_values(splits[1], (TOTAL, D), (1.22 * D ** -0.25), 1.253025, ((0, 16),), jnp.float32)
    labels = jax.random.permutation(splits[2], TOTAL).astype(jnp.int32)
    return dict(images=images, texts=texts, labels=labels)


logit_bias = -6.0


def reference(images, texts, labels):
    total = images.shape[0]
    width = images.shape[1]
    count = total // ROWS_DEV
    image_low = lax.optimization_barrier(images.astype(jnp.bfloat16)).astype(jnp.float32)
    text_low = lax.optimization_barrier(texts.astype(jnp.bfloat16)).astype(jnp.float32)
    image_blocks = image_low.reshape(count, ROWS_DEV, width)
    label_blocks = labels.reshape(count, ROWS_DEV)
    columns = jnp.arange(total, dtype=jnp.int32)

    def one_block(text_total, piece):
        image_piece, label_piece = piece
        logits = jnp.dot(image_piece, text_low.T, preferred_element_type=jnp.float32) + logit_bias
        positive = (label_piece[:, None] == columns[None, :]).astype(jnp.float32)
        weights = (jax.nn.sigmoid(logits) - positive).astype(jnp.bfloat16)
        weights = lax.optimization_barrier(weights).astype(jnp.float32)
        image_part = jnp.dot(weights, text_low, preferred_element_type=jnp.float32)
        text_total = text_total + jnp.dot(weights.T, image_piece, preferred_element_type=jnp.float32)
        return text_total, image_part

    text_grad, image_parts = lax.scan(one_block, jnp.zeros((total, width), jnp.float32), (image_blocks, label_blocks))
    return image_parts.reshape(total, width), text_grad
```

```python
import functools

import jax
import jax.numpy as jnp
from jax import lax
from jax.experimental import pallas as pl
from jax.experimental.pallas import tpu as pltpu
from jax.sharding import PartitionSpec as P

logit_bias = -6.0
MESH = pl.DeviceIdType.MESH
F32 = jnp.float32
BF16 = jnp.bfloat16


def kernel(
    planes, lanes, parts, pieces, cuts,
    images, texts, labels, image_out, text_out,
    img, txt, lab, acc, own, above, below, passing, c_out, c_in, x_out, x_in, y_out, y_in, kept,
    local_sem, i_send, i_recv, fx_send, fy_send, fc_send, f_recv, n_recv,
    l_send, l_recv, t_up, t_down, t_recv,
    g_send, a_recv, b_recv, c_send, c_recv, x_send, x_recv, y_send, y_recv,
):
    rows = images.shape[0]
    share = rows // lanes
    cut = share // cuts
    fine = share // pieces
    part = share // parts
    chunks = 2 * lanes
    tall = rows // chunks
    block = lax.axis_index("block")
    y = lax.axis_index("lane")
    p, x, c = block // 4, (block // 2) % 2, block % 2

    def at(plane, xx, cc, lane=None):
        return {"block": plane * 4 + xx * 2 + cc, "lane": y if lane is None else lane}

    def remote(src, dst, send, recv, device):
        return pltpu.make_async_remote_copy(
            src_ref=src, dst_ref=dst, send_sem=send, recv_sem=recv, device_id=device, device_id_type=MESH
        )

    other_core, other_x, corner = at(p, x, 1 - c), at(p, 1 - x, c), at(p, 1 - x, 1 - c)
    has_up, has_down = p < planes - 1, p > 0
    up, down = at(p + 1, x, c), at(p - 1, x, c)

    def block_rows(index):
        return pl.ds(pl.multiple_of(index * rows, rows), rows)

    mine = x * 2 + c
    far = (1 - x) * 2 + c

    barrier = pltpu.get_barrier_semaphore()

    def greet(device):
        pl.semaphore_signal(barrier, inc=1, device_id=device, device_id_type=MESH)

    greet(other_core)
    greet(other_x)
    greet(corner)
    for step in range(1, lanes):
        greet(at(p, x, c, lax.rem(y + step, lanes)))

    @pl.when(has_up)
    def _():
        greet(up)

    @pl.when(has_down)
    def _():
        greet(down)

    load_txt = pltpu.make_async_copy(
        texts.at[pl.ds(pl.multiple_of(y * share, share), share)], own.at[0], local_sem.at[1]
    )
    load_img = pltpu.make_async_copy(images, acc.at[pl.ds(0, rows)], local_sem.at[0])
    keep_lab = pltpu.make_async_copy(labels, lab.at[mine], local_sem.at[2])
    load_txt.start()
    load_img.start()
    keep_lab.start()
    load_txt.wait()
    txt[p] = own[0].astype(BF16)
    pl.semaphore_wait(barrier, 2 + lanes + has_up.astype(jnp.int32) + has_down.astype(jnp.int32))

    def text_copy(q, half, going_up):
        spot = txt.at[q, pl.ds(pl.multiple_of(half * cut, cut), cut)]
        index = q * cuts + half
        return remote(
            spot, spot, (t_up if going_up else t_down).at[index], t_recv.at[index], up if going_up else down
        )

    @pl.when(has_up)
    def _():
        for half in range(cuts):
            text_copy(p, half, True).start()

    @pl.when(has_down)
    def _():
        for half in range(cuts):
            text_copy(p, half, False).start()

    def text_passes(t, half):
        low, high = p - t, p + t

        @pl.when((low >= 0) & has_up)
        def _():
            text_copy(low, half, True).wait_recv()
            text_copy(low, half, True).start()

        @pl.when((high < planes) & has_down)
        def _():
            text_copy(high, half, False).wait_recv()
            text_copy(high, half, False).start()

    def text_stays(t, half):
        low, high = p - t, p + t

        @pl.when((low >= 0) & jnp.logical_not(has_up))
        def _():
            text_copy(low, half, True).wait_recv()

        @pl.when((high < planes) & jnp.logical_not(has_down))
        def _():
            text_copy(high, half, False).wait_recv()

    image_near = remote(img.at[block_rows(mine)], img.at[block_rows(mine)], i_send.at[0], i_recv.at[0], other_core)

    def piece_rows(index, lane, piece):
        return pl.ds(pl.multiple_of(index * rows + lane * share + piece * fine, fine), fine)

    def far_x(piece):
        spot = img.at[piece_rows(mine, y, piece)]
        return remote(
            spot, spot, fx_send.at[piece], f_recv.at[y * pieces + piece], other_x
        )

    def far_y(step, piece):
        spot = img.at[piece_rows(far, y, piece)]
        device = at(p, x, c, lax.rem(y + step, lanes))
        return remote(spot, spot, fy_send.at[step * pieces + piece], f_recv.at[y * pieces + piece], device)

    def far_core(lane, piece):
        spot = img.at[piece_rows(far, lane, piece)]
        return remote(spot, spot, fc_send.at[lane * pieces + piece], n_recv.at[lane * pieces + piece], other_core)

    def far_arrived(lane, piece):
        spot = img.at[piece_rows(far, lane, piece)]
        return remote(spot, spot, fx_send.at[piece], f_recv.at[lane * pieces + piece], other_x)
    label_copies = [
        remote(labels, lab.at[mine], l_send.at[k], l_recv.at[k], device)
        for k, device in enumerate((other_core, other_x, corner))
    ]
    for copy in label_copies:
        copy.start()
    load_img.wait()
    img[block_rows(mine)] = acc[pl.ds(0, rows)].astype(BF16)
    for piece in range(pieces):
        far_x(piece).start()
    image_near.start()
    acc[...] = jnp.zeros_like(acc)
    own[...] = jnp.zeros_like(own)
    keep_lab.wait()
    for copy in label_copies:
        copy.wait_recv()
    image_near.wait_recv()

    def compute(q, xx):
        text_now = txt[q]
        first = (q * 4 + x * 2 + c) * rows + y * share
        text_ids = first + lax.broadcasted_iota(jnp.int32, (share, rows), 0)
        for cc in range(2):
            index = xx * 2 + cc
            image_now = img[block_rows(index)]
            logits = lax.dot_general(
                text_now, image_now, (((1,), (1,)), ((), ())), preferred_element_type=F32
            ) + logit_bias
            positive = (lab[index] == text_ids).astype(F32)
            weights = (jax.nn.sigmoid(logits) - positive).astype(BF16)
            own[q] += jnp.dot(weights, image_now, preferred_element_type=F32)
            acc[block_rows(index)] += lax.dot_general(
                weights, text_now, (((0,), (0,)), ((), ())), preferred_element_type=F32
            )

    def pass_to_core(piece):
        for step in range(1, lanes):
            lane = lax.rem(y + step, lanes)
            far_arrived(lane, piece).wait_recv()
            far_core(lane, piece).start()

    def gather(piece, carry):
        far_arrived(y, piece).wait_recv()
        for step in range(1, lanes):
            far_y(step, piece).start()
        far_core(y, piece).start()

        def text_pieces(half, carry):
            text_passes(1, half)
            text_stays(1, half)
            return carry

        lax.fori_loop(piece * cuts // pieces, (piece + 1) * cuts // pieces, text_pieces, 0)

        @pl.when(piece == 0)
        def _():
            compute(p, x)

        @pl.when(piece > 0)
        def _():
            pass_to_core(piece - 1)

        return carry

    lax.fori_loop(0, pieces, gather, 0)

    last_compute = jnp.maximum(p, planes - 1 - p)

    def grad_copy(q, k, going_up):
        spot = (q, pl.ds(pl.multiple_of(k * part, part), part))
        index = q * parts + k
        return remote(
            passing.at[spot], (below if going_up else above).at[spot], g_send.at[index],
            (b_recv if going_up else a_recv).at[index], up if going_up else down,
        )

    def chunk_rows(m):
        return pl.ds(pl.multiple_of(m * tall, tall), tall)

    def c_copy(xx, m):
        index = xx * chunks + m
        return remote(
            c_out.at[xx, chunk_rows(m)], c_in.at[xx, chunk_rows(m)], c_send.at[index], c_recv.at[index], other_core
        )

    def x_copy(m):
        index = jnp.int32(m)
        return remote(
            x_out.at[chunk_rows(index)], x_in.at[chunk_rows(index)], x_send.at[index], x_recv.at[index], other_x
        )

    def y_copy(lane, kind):
        slot = lax.rem(lane - y + lanes, lanes)
        index = slot * 3 + kind
        return remote(y_out.at[index], y_in.at[index], y_send.at[index], y_recv.at[index], at(p, x, c, lane))

    def acc_rows(index, m):
        return pl.ds(pl.multiple_of(index * rows + m * tall, tall), tall)

    toward = jnp.where(2 * p < planes, 1, -1)
    own_step = min(2, planes - 1)
    far_item = 3 if planes > 2 else 0
    ends_last = last_compute == planes - 1
    lag = 3
    at_first_hop = last_compute * (parts + lag) + jnp.where(ends_last, 0, 1)
    at_second_hop = jnp.where(ends_last, last_compute, last_compute + 1) * (parts + lag)
    at_last_hop = at_second_hop + jnp.where(ends_last, parts // 2, parts // 4)

    def one_step(t, carry):
        def one_item(i, carry):
            q = jnp.where(i == 0, p, jnp.where(i % 2 == 1, p + toward * t, p - toward * t))
            xx = jnp.where((i == 1) | (i == 2), x, 1 - x)
            valid = jnp.where(i == 0, t == own_step, (q >= 0) & (q < planes))

            @pl.when((t == 1) & (i == min(2, far_item)))
            def _():
                pass_to_core(pieces - 1)

            @pl.when((t == 1) & (i == far_item))
            def _():
                for piece in range(pieces):
                    for step in range(lanes):
                        far_core(lax.rem(y + step, lanes), piece).wait_recv()

            @pl.when((t > 1) & (i == 1))
            def _():
                for half in range(cuts):
                    text_stays(t, half)

            @pl.when(valid)
            def _():
                compute(q, xx)

            @pl.when(i > 0)
            def _():
                def pass_on(half, carry):
                    text_passes(t + 1, half)
                    return carry

                lax.fori_loop((i - 1) * cuts // 4, i * cuts // 4, pass_on, 0)

            return carry

        lax.fori_loop(0, 5, one_item, 0)

        @pl.when(t == last_compute)
        def _():
            def send(n, carry):
                half, xx = n // (2 * lanes), jnp.where((n // lanes) % 2 == 0, 1 - x, x)
                m = lax.rem(y + 1 + n, lanes) * 2 + half
                c_out[xx, chunk_rows(m)] = acc[acc_rows(xx * 2 + 1 - c, m)].astype(BF16)
                c_copy(xx, m).start()
                return carry

            lax.fori_loop(0, 4 * lanes, send, 0)

        def first_hop(n, carry):
            lane = lax.rem(y + 1 + n, lanes)
            m = lane * 2
            c_copy(1 - x, m).wait_recv()
            x_out[chunk_rows(m)] = (
                acc[acc_rows(far, m)] + c_in[1 - x, chunk_rows(m)].astype(F32)
            ).astype(BF16)
            x_copy(m).start()

            @pl.when(lane != y)
            def _():
                def second_halves(k, carry):
                    xx = jnp.where(k == 0, 1 - x, x)
                    c_copy(xx, m + 1).wait_recv()
                    y_out[lax.rem(lane - y + lanes, lanes) * 3 + 1 + xx] = (
                        acc[acc_rows(xx * 2 + c, m + 1)] + c_in[xx, chunk_rows(m + 1)].astype(F32)
                    ).astype(BF16)
                    y_copy(lane, 1 + xx).start()
                    return carry

                lax.fori_loop(0, 2, second_halves, 0)

            return carry

        def second_hop(n, carry):
            lane = lax.rem(y + 1 + n, lanes)
            m = lane * 2
            c_copy(x, m).wait_recv()
            x_copy(m).wait_recv()
            total = (
                acc[acc_rows(mine, m)] + c_in[x, chunk_rows(m)].astype(F32) + x_in[chunk_rows(m)].astype(F32)
            )

            @pl.when(lane == y)
            def _():
                kept[pl.ds(0, tall)] = total

            @pl.when(lane != y)
            def _():
                y_out[lax.rem(lane - y + lanes, lanes) * 3] = total.astype(BF16)
                y_copy(lane, 0).start()

            return carry

        def gathered(xx):
            m = y * 2 + 1
            c_copy(xx, m).wait_recv()
            total = acc[acc_rows(xx * 2 + c, m)] + c_in[xx, chunk_rows(m)].astype(F32)
            for step in range(1, lanes):
                y_copy(lax.rem(y + step, lanes), 1 + xx).wait_recv()
                total = total + y_in[step * 3 + 1 + xx].astype(F32)
            return total

        def send_last():
            x_out[chunk_rows(1)] = gathered(1 - x).astype(BF16)
            x_copy(1).start()

        def grad_start(q, going_up):
            def one_part(k, carry):
                spot = (q, pl.ds(pl.multiple_of(k * part, part), part))
                passing[spot] = own[spot].astype(BF16)
                grad_copy(q, k, going_up).start()
                return carry

            lax.fori_loop(0, parts, one_part, 0)

        @pl.when(p == 0)
        def _():
            grad_start(t, True)

        @pl.when(p == planes - 1)
        def _():
            grad_start(planes - 1 - t, False)

        def one_part(k, carry):
            at_now = t * (parts + lag) + k
            k_up = k - jnp.where(2 * p < planes, 0, lag)
            k_down = k - jnp.where(2 * p < planes, lag, 0)

            @pl.when(at_now == at_first_hop)
            def _():
                lax.fori_loop(0, lanes, first_hop, 0)

            @pl.when(at_now == at_second_hop)
            def _():
                lax.fori_loop(0, lanes - 1, second_hop, 0)
                send_last()

            @pl.when(at_now == at_last_hop)
            def _():
                lax.fori_loop(lanes - 1, lanes, second_hop, 0)
                kept[pl.ds(tall, tall)] = gathered(x)

            def spot_of(q, k):
                return (q, pl.ds(pl.multiple_of(k * part, part), part))

            @pl.when((t > p) & has_down & (k_up >= 0) & (k_up < parts))
            def _():
                spot = spot_of(t, k_up)
                grad_copy(t, k_up, True).wait_recv()
                passing[spot] = (own[spot] + below[spot].astype(F32)).astype(BF16)
                grad_copy(t, k_up, True).start()

            q_above = planes - 1 - t

            @pl.when((q_above < p) & has_up & (k_down >= 0) & (k_down < parts))
            def _():
                spot = spot_of(q_above, k_down)
                grad_copy(q_above, k_down, False).wait_recv()
                passing[spot] = (own[spot] + above[spot].astype(F32)).astype(BF16)
                grad_copy(q_above, k_down, False).start()

            @pl.when((t == planes - 1) & (k < parts))
            def _():
                spot = spot_of(p, k)

                @pl.when(has_down)
                def _():
                    grad_copy(p, k, True).wait_recv()
                    own[spot] += below[spot].astype(F32)

                @pl.when(has_up)
                def _():
                    grad_copy(p, k, False).wait_recv()
                    own[spot] += above[spot].astype(F32)

            return carry

        lax.fori_loop(0, parts + lag, one_part, 0)

        return carry

    lax.fori_loop(1, planes, one_step, 0)

    text_out[...] = own[p]
    first_half = kept[pl.ds(0, tall)]
    for step in range(1, lanes):
        y_copy(lax.rem(y + step, lanes), 0).wait_recv()
        first_half = first_half + y_in[step * 3].astype(F32)
    image_out[pl.ds(0, tall)] = first_half
    x_copy(1).wait_recv()
    image_out[pl.ds(tall, tall)] = kept[pl.ds(tall, tall)] + x_in[chunk_rows(1)].astype(F32)
    for step in range(1, lanes):
        for kind in range(3):
            y_copy(lax.rem(y + step, lanes), kind).wait_send()
    for piece in range(pieces):
        far_x(piece).wait_send()
        for step in range(lanes):
            far_core(lax.rem(y + step, lanes), piece).wait_send()
            if step > 0:
                far_y(step, piece).wait_send()
    x_copy(1).wait_send()
    image_near.wait_send()
    for copy in label_copies:
        copy.wait_send()

    def settle(q, carry):
        @pl.when((q <= p) & has_up)
        def _():
            for half in range(cuts):
                text_copy(q, half, True).wait_send()

        @pl.when((q >= p) & has_down)
        def _():
            for half in range(cuts):
                text_copy(q, half, False).wait_send()

        @pl.when(q != p)
        def _():
            def one_part(k, carry):
                grad_copy(q, k, True).wait_send()
                return carry

            lax.fori_loop(0, parts, one_part, 0)

        return carry

    lax.fori_loop(0, planes, settle, 0)

    def settle_chunks(m, carry):
        c_copy(0, m).wait_send()
        c_copy(1, m).wait_send()

        @pl.when(m % 2 == 0)
        def _():
            x_copy(m).wait_send()

        return carry

    lax.fori_loop(0, chunks, settle_chunks, 0)


def solution(mesh):
    lanes = mesh.shape["lane"]
    planes = mesh.shape["block"] // 4
    pieces, cuts = 4, 4

    def on_device(images, texts, labels):
        rows, width = images.shape
        share = rows // lanes
        parts = min(8, share // 16)
        chunks = 2 * lanes
        dma = lambda n: pltpu.SemaphoreType.DMA((n,))
        hbm = pl.BlockSpec(memory_space=pl.ANY)
        vmem = pl.BlockSpec(memory_space=pltpu.VMEM)
        half = lambda *s: pltpu.VMEM(s, BF16)
        full = lambda *s: pltpu.VMEM(s, F32)
        return pl.pallas_call(
            functools.partial(kernel, planes, lanes, parts, pieces, cuts),
            out_shape=(
                jax.ShapeDtypeStruct((share, width), F32),
                jax.ShapeDtypeStruct((share, width), F32),
            ),
            in_specs=[hbm, hbm, hbm],
            out_specs=(vmem, vmem),
            scratch_shapes=[
                half(4 * rows, width),
                half(planes, share, width),
                pltpu.VMEM((4, 1, rows), jnp.int32),
                full(4 * rows, width),
                full(planes, share, width),
                half(planes, share, width),
                half(planes, share, width),
                half(planes, share, width),
                half(2, rows, width),
                half(2, rows, width),
                half(rows, width),
                half(rows, width),
                half(3 * lanes, share // 2, width),
                half(3 * lanes, share // 2, width),
                full(share, width),
                dma(3), dma(1), dma(1), dma(pieces), *[dma(lanes * pieces)] * 4,
                dma(3), dma(3), *[dma(cuts * planes)] * 3,
                dma(planes * parts), dma(planes * parts), dma(planes * parts),
                dma(2 * chunks), dma(2 * chunks), dma(chunks), dma(chunks), dma(3 * lanes), dma(3 * lanes),
            ],
            compiler_params=pltpu.CompilerParams(
                collective_id=0, has_side_effects=True, vmem_limit_bytes=62 * 1024 * 1024
            ),
        )(images, texts, labels.reshape(1, rows))

    return jax.shard_map(
        on_device,
        mesh=mesh,
        in_specs=(P("block", None), P("block", None), P("block")),
        out_specs=(P(("block", "lane"), None), P(("block", "lane"), None)),
        check_vma=False,
    )
```

```python
import functools

import jax
import jax.numpy as jnp
from jax import lax
from jax.experimental import pallas as pl
from jax.experimental.pallas import tpu as pltpu
from jax.sharding import PartitionSpec as P

logit_bias = -6.0
MESH = pl.DeviceIdType.MESH
F32 = jnp.float32
BF16 = jnp.bfloat16


def kernel(
    planes, lanes, parts, pieces, cuts,
    images, texts, labels, image_out, text_out,
    img, txt, lab, acc, own, above, below, passing, c_out, c_in, x_out, x_in, y_out, y_in, kept,
    local_sem, i_send, i_recv, fx_send, fy_send, fc_send, f_recv, n_recv,
    l_send, l_recv, t_up, t_down, t_recv,
    g_send, a_recv, b_recv, c_send, c_recv, x_send, x_recv, y_send, y_recv,
):
    rows = images.shape[0]
    share = rows // lanes
    cut = share // cuts
    fine = share // pieces
    part = share // parts
    chunks = 2 * lanes
    tall = rows // chunks
    block = lax.axis_index("block")
    y = lax.axis_index("lane")
    p, x, c = block // 4, (block // 2) % 2, block % 2

    def at(plane, xx, cc, lane=None):
        return {"block": plane * 4 + xx * 2 + cc, "lane": y if lane is None else lane}

    def remote(src, dst, send, recv, device):
        return pltpu.make_async_remote_copy(
            src_ref=src, dst_ref=dst, send_sem=send, recv_sem=recv, device_id=device, device_id_type=MESH
        )

    other_core, other_x, corner = at(p, x, 1 - c), at(p, 1 - x, c), at(p, 1 - x, 1 - c)
    has_up, has_down = p < planes - 1, p > 0
    up, down = at(p + 1, x, c), at(p - 1, x, c)

    def block_rows(index):
        return pl.ds(pl.multiple_of(index * rows, rows), rows)

    mine = x * 2 + c
    far = (1 - x) * 2 + c

    barrier = pltpu.get_barrier_semaphore()

    def greet(device):
        pl.semaphore_signal(barrier, inc=1, device_id=device, device_id_type=MESH)

    greet(other_core)
    greet(other_x)
    greet(corner)
    for step in range(1, lanes):
        greet(at(p, x, c, lax.rem(y + step, lanes)))

    @pl.when(has_up)
    def _():
        greet(up)

    @pl.when(has_down)
    def _():
        greet(down)

    load_txt = pltpu.make_async_copy(
        texts.at[pl.ds(pl.multiple_of(y * share, share), share)], own.at[0], local_sem.at[1]
    )
    load_img = pltpu.make_async_copy(images, acc.at[pl.ds(0, rows)], local_sem.at[0])
    keep_lab = pltpu.make_async_copy(labels, lab.at[mine], local_sem.at[2])
    load_txt.start()
    load_img.start()
    keep_lab.start()
    load_txt.wait()
    txt[p] = own[0].astype(BF16)
    pl.semaphore_wait(barrier, 2 + lanes + has_up.astype(jnp.int32) + has_down.astype(jnp.int32))

    def text_copy(q, half, going_up):
        spot = txt.at[q, pl.ds(pl.multiple_of(half * cut, cut), cut)]
        index = q * cuts + half
        return remote(
            spot, spot, (t_up if going_up else t_down).at[index], t_recv.at[index], up if going_up else down
        )

    @pl.when(has_up)
    def _():
        for half in range(cuts):
            text_copy(p, half, True).start()

    @pl.when(has_down)
    def _():
        for half in range(cuts):
            text_copy(p, half, False).start()

    def text_passes(t, half):
        low, high = p - t, p + t

        @pl.when((low >= 0) & has_up)
        def _():
            text_copy(low, half, True).wait_recv()
            text_copy(low, half, True).start()

        @pl.when((high < planes) & has_down)
        def _():
            text_copy(high, half, False).wait_recv()
            text_copy(high, half, False).start()

    def text_stays(t, half):
        low, high = p - t, p + t

        @pl.when((low >= 0) & jnp.logical_not(has_up))
        def _():
            text_copy(low, half, True).wait_recv()

        @pl.when((high < planes) & jnp.logical_not(has_down))
        def _():
            text_copy(high, half, False).wait_recv()

    image_near = remote(img.at[block_rows(mine)], img.at[block_rows(mine)], i_send.at[0], i_recv.at[0], other_core)

    def piece_rows(index, lane, piece):
        return pl.ds(pl.multiple_of(index * rows + lane * share + piece * fine, fine), fine)

    def far_x(piece):
        spot = img.at[piece_rows(mine, y, piece)]
        return remote(
            spot, spot, fx_send.at[piece], f_recv.at[y * pieces + piece], other_x
        )

    def far_y(step, piece):
        spot = img.at[piece_rows(far, y, piece)]
        device = at(p, x, c, lax.rem(y + step, lanes))
        return remote(spot, spot, fy_send.at[step * pieces + piece], f_recv.at[y * pieces + piece], device)

    def far_core(lane, piece):
        spot = img.at[piece_rows(far, lane, piece)]
        return remote(spot, spot, fc_send.at[lane * pieces + piece], n_recv.at[lane * pieces + piece], other_core)

    def far_arrived(lane, piece):
        spot = img.at[piece_rows(far, lane, piece)]
        return remote(spot, spot, fx_send.at[piece], f_recv.at[lane * pieces + piece], other_x)
    label_copies = [
        remote(labels, lab.at[mine], l_send.at[k], l_recv.at[k], device)
        for k, device in enumerate((other_core, other_x, corner))
    ]
    for copy in label_copies:
        copy.start()
    load_img.wait()
    img[block_rows(mine)] = acc[pl.ds(0, rows)].astype(BF16)
    for piece in range(pieces):
        far_x(piece).start()
    image_near.start()
    acc[...] = jnp.zeros_like(acc)
    own[...] = jnp.zeros_like(own)
    keep_lab.wait()
    for copy in label_copies:
        copy.wait_recv()
    image_near.wait_recv()

    def tile(q, index, start, height):
        spot = (q, pl.ds(pl.multiple_of(start, height), height))
        text_now = txt[spot]
        first = (q * 4 + x * 2 + c) * rows + y * share + start
        text_ids = first + lax.broadcasted_iota(jnp.int32, (height, rows), 0)
        image_now = img[block_rows(index)]
        logits = lax.dot_general(
            text_now, image_now, (((1,), (1,)), ((), ())), preferred_element_type=F32
        ) + logit_bias
        positive = (lab[index] == text_ids).astype(F32)
        weights = (jax.nn.sigmoid(logits) - positive).astype(BF16)
        own[spot] += jnp.dot(weights, image_now, preferred_element_type=F32)
        acc[block_rows(index)] += lax.dot_general(
            weights, text_now, (((0,), (0,)), ((), ())), preferred_element_type=F32
        )

    def compute(q, xx):
        for cc in range(2):
            tile(q, xx * 2 + cc, 0, share)

    def pass_to_core(piece):
        for step in range(1, lanes):
            lane = lax.rem(y + step, lanes)
            far_arrived(lane, piece).wait_recv()
            far_core(lane, piece).start()

    def gather(piece, carry):
        far_arrived(y, piece).wait_recv()
        for step in range(1, lanes):
            far_y(step, piece).start()
        far_core(y, piece).start()

        def text_pieces(half, carry):
            text_passes(1, half)
            text_stays(1, half)
            return carry

        lax.fori_loop(piece * cuts // pieces, (piece + 1) * cuts // pieces, text_pieces, 0)

        @pl.when(piece == 0)
        def _():
            compute(p, x)

        @pl.when(piece > 0)
        def _():
            pass_to_core(piece - 1)

        return carry

    lax.fori_loop(0, pieces, gather, 0)

    last_compute = jnp.maximum(p, planes - 1 - p)

    def grad_copy(q, k, going_up):
        spot = (q, pl.ds(pl.multiple_of(k * part, part), part))
        index = q * parts + k
        return remote(
            passing.at[spot], (below if going_up else above).at[spot], g_send.at[index],
            (b_recv if going_up else a_recv).at[index], up if going_up else down,
        )

    def chunk_rows(m):
        return pl.ds(pl.multiple_of(m * tall, tall), tall)

    def c_copy(xx, m):
        index = xx * chunks + m
        return remote(
            c_out.at[xx, chunk_rows(m)], c_in.at[xx, chunk_rows(m)], c_send.at[index], c_recv.at[index], other_core
        )

    def x_copy(m):
        index = jnp.int32(m)
        return remote(
            x_out.at[chunk_rows(index)], x_in.at[chunk_rows(index)], x_send.at[index], x_recv.at[index], other_x
        )

    def y_copy(lane, kind):
        slot = lax.rem(lane - y + lanes, lanes)
        index = slot * 3 + kind
        return remote(y_out.at[index], y_in.at[index], y_send.at[index], y_recv.at[index], at(p, x, c, lane))

    def acc_rows(index, m):
        return pl.ds(pl.multiple_of(index * rows + m * tall, tall), tall)

    toward = jnp.where(2 * p < planes, 1, -1)
    own_step = min(2, planes - 1)
    far_item = 3 if planes > 2 else 0
    ends_last = last_compute == planes - 1
    lag = 3
    early = parts * 5 // 8
    at_first_hop = last_compute * (parts + lag) + jnp.where(ends_last, 0, 1)
    at_second_hop = jnp.where(ends_last, last_compute, last_compute + 1) * (parts + lag)
    at_last_hop = at_second_hop + jnp.where(ends_last, 1, parts + lag - 1)

    def one_step(t, carry):
        apart = ends_last & (t == planes - 1)

        def one_item(i, carry):
            q = jnp.where(i == 0, p, jnp.where(i % 2 == 1, p + toward * t, p - toward * t))
            xx = jnp.where((i == 1) | (i == 2), x, 1 - x)
            valid = jnp.where(i == 0, t == own_step, (q >= 0) & (q < planes) & jnp.logical_not(apart))

            @pl.when((t == 1) & (i == min(2, far_item)))
            def _():
                pass_to_core(pieces - 1)

            @pl.when((t == 1) & (i == far_item))
            def _():
                for piece in range(pieces):
                    for step in range(lanes):
                        far_core(lax.rem(y + step, lanes), piece).wait_recv()

            @pl.when((t > 1) & (i == 1) & jnp.logical_not(apart))
            def _():
                for half in range(cuts):
                    text_stays(t, half)

            @pl.when(valid)
            def _():
                compute(q, xx)

            @pl.when(i > 0)
            def _():
                def pass_on(half, carry):
                    text_passes(t + 1, half)
                    return carry

                lax.fori_loop((i - 1) * cuts // 4, i * cuts // 4, pass_on, 0)

            return carry

        lax.fori_loop(0, 5, one_item, 0)

        def send_to_core():
            def send(n, carry):
                half, xx = n // (2 * lanes), jnp.where((n // lanes) % 2 == 0, 1 - x, x)
                m = lax.rem(y + 1 + n, lanes) * 2 + half
                c_out[xx, chunk_rows(m)] = acc[acc_rows(xx * 2 + 1 - c, m)].astype(BF16)
                c_copy(xx, m).start()
                return carry

            lax.fori_loop(0, 4 * lanes, send, 0)

        @pl.when((t == last_compute) & jnp.logical_not(ends_last))
        def _():
            send_to_core()

        def first_hop(n, carry):
            lane = lax.rem(y + 1 + n, lanes)
            m = lane * 2
            c_copy(1 - x, m).wait_recv()
            x_out[chunk_rows(m)] = (
                acc[acc_rows(far, m)] + c_in[1 - x, chunk_rows(m)].astype(F32)
            ).astype(BF16)
            x_copy(m).start()

            @pl.when(lane != y)
            def _():
                def second_halves(k, carry):
                    xx = jnp.where(k == 0, 1 - x, x)
                    c_copy(xx, m + 1).wait_recv()
                    y_out[lax.rem(lane - y + lanes, lanes) * 3 + 1 + xx] = (
                        acc[acc_rows(xx * 2 + c, m + 1)] + c_in[xx, chunk_rows(m + 1)].astype(F32)
                    ).astype(BF16)
                    y_copy(lane, 1 + xx).start()
                    return carry

                lax.fori_loop(0, 2, second_halves, 0)

            return carry

        def second_hop(n, carry):
            lane = lax.rem(y + 1 + n, lanes)
            m = lane * 2
            c_copy(x, m).wait_recv()
            x_copy(m).wait_recv()
            total = (
                acc[acc_rows(mine, m)] + c_in[x, chunk_rows(m)].astype(F32) + x_in[chunk_rows(m)].astype(F32)
            )

            @pl.when(lane == y)
            def _():
                kept[pl.ds(0, tall)] = total

            @pl.when(lane != y)
            def _():
                y_out[lax.rem(lane - y + lanes, lanes) * 3] = total.astype(BF16)
                y_copy(lane, 0).start()

            return carry

        def gathered(xx):
            m = y * 2 + 1
            c_copy(xx, m).wait_recv()
            total = acc[acc_rows(xx * 2 + c, m)] + c_in[xx, chunk_rows(m)].astype(F32)
            for step in range(1, lanes):
                y_copy(lax.rem(y + step, lanes), 1 + xx).wait_recv()
                total = total + y_in[step * 3 + 1 + xx].astype(F32)
            return total

        def send_last():
            x_out[chunk_rows(1)] = gathered(1 - x).astype(BF16)
            x_copy(1).start()

        def grad_start(q, going_up, first, last):
            def one_part(k, carry):
                spot = (q, pl.ds(pl.multiple_of(k * part, part), part))
                passing[spot] = own[spot].astype(BF16)
                grad_copy(q, k, going_up).start()
                return carry

            lax.fori_loop(first, last, one_part, 0)

        def grad_starts(t, first, last):
            @pl.when(p == 0)
            def _():
                grad_start(t, True, first, last)

            @pl.when(p == planes - 1)
            def _():
                grad_start(planes - 1 - t, False, first, last)

        @pl.when(ends_last & (t < planes - 1))
        def _():
            grad_starts(t, 0, jnp.where(t == 1, early, parts))

        @pl.when(apart)
        def _():
            def one_slice(h, carry):
                def arrive(half, carry):
                    text_stays(t, half)
                    return carry

                lax.fori_loop(h * cuts // 2, (h + 1) * cuts // 2, arrive, 0)

                def one_tile(n, carry):
                    index = jnp.where(n % 2 == 0, 1 - x, x) * 2 + jnp.where(n < 2, 1 - c, c)
                    tile(p + toward * t, index, h * (share // 2), share // 2)

                    @pl.when((h == 1) & (n == 1))
                    def _():
                        send_to_core()

                    return carry

                lax.fori_loop(0, 4, one_tile, 0)
                grad_starts(t, h * parts // 2, (h + 1) * parts // 2)
                return carry

            lax.fori_loop(0, 2, one_slice, 0)
            grad_starts(jnp.int32(1), early, parts)

        def one_part(k, carry):
            at_now = t * (parts + lag) + k
            k_up = k - jnp.where(2 * p < planes, 0, lag)
            k_down = k - jnp.where(2 * p < planes, lag, 0)

            @pl.when(at_now == at_first_hop)
            def _():
                lax.fori_loop(0, lanes, first_hop, 0)

            @pl.when(at_now == at_second_hop)
            def _():
                lax.fori_loop(0, lanes - 1, second_hop, 0)
                send_last()

            @pl.when(at_now == at_last_hop)
            def _():
                lax.fori_loop(lanes - 1, lanes, second_hop, 0)
                kept[pl.ds(tall, tall)] = gathered(x)

            def spot_of(q, k):
                return (q, pl.ds(pl.multiple_of(k * part, part), part))

            @pl.when((t > p) & has_down & (k_up >= 0) & (k_up < parts))
            def _():
                spot = spot_of(t, k_up)
                grad_copy(t, k_up, True).wait_recv()
                passing[spot] = (own[spot] + below[spot].astype(F32)).astype(BF16)
                grad_copy(t, k_up, True).start()

            q_above = planes - 1 - t

            @pl.when((q_above < p) & has_up & (k_down >= 0) & (k_down < parts))
            def _():
                spot = spot_of(q_above, k_down)
                grad_copy(q_above, k_down, False).wait_recv()
                passing[spot] = (own[spot] + above[spot].astype(F32)).astype(BF16)
                grad_copy(q_above, k_down, False).start()

            return carry

        lax.fori_loop(0, parts + lag, one_part, 0)

        return carry

    lax.fori_loop(1, planes, one_step, 0)

    for piece in range(pieces):
        far_x(piece).wait_send()
        for step in range(lanes):
            far_core(lax.rem(y + step, lanes), piece).wait_send()
            if step > 0:
                far_y(step, piece).wait_send()
    image_near.wait_send()
    for copy in label_copies:
        copy.wait_send()

    def settle(q, carry):
        @pl.when((q <= p) & has_up)
        def _():
            for half in range(cuts):
                text_copy(q, half, True).wait_send()

        @pl.when((q >= p) & has_down)
        def _():
            for half in range(cuts):
                text_copy(q, half, False).wait_send()

        return carry

    lax.fori_loop(0, planes, settle, 0)

    def last_sums(k, carry):
        spot = (p, pl.ds(pl.multiple_of(k * part, part), part))

        @pl.when(has_up)
        def _():
            grad_copy(p, k, False).wait_recv()
            own[spot] += above[spot].astype(F32)

        @pl.when(has_down)
        def _():
            grad_copy(p, k, True).wait_recv()
            own[spot] += below[spot].astype(F32)

        return carry

    lax.fori_loop(0, parts, last_sums, 0)
    save_text = pltpu.make_async_copy(own.at[p], text_out, local_sem.at[1])
    save_text.start()
    first_half = kept[pl.ds(0, tall)]
    for step in range(1, lanes):
        y_copy(lax.rem(y + step, lanes), 0).wait_recv()
        first_half = first_half + y_in[step * 3].astype(F32)
    kept[pl.ds(0, tall)] = first_half
    x_copy(1).wait_recv()
    kept[pl.ds(tall, tall)] += x_in[chunk_rows(1)].astype(F32)
    save_image = pltpu.make_async_copy(kept, image_out, local_sem.at[0])
    save_image.start()
    for step in range(1, lanes):
        for kind in range(3):
            y_copy(lax.rem(y + step, lanes), kind).wait_send()
    x_copy(1).wait_send()

    def settle_grads(q, carry):
        @pl.when(q != p)
        def _():
            def one_part(k, carry):
                grad_copy(q, k, True).wait_send()
                return carry

            lax.fori_loop(0, parts, one_part, 0)

        return carry

    lax.fori_loop(0, planes, settle_grads, 0)

    def settle_chunks(m, carry):
        c_copy(0, m).wait_send()
        c_copy(1, m).wait_send()

        @pl.when(m % 2 == 0)
        def _():
            x_copy(m).wait_send()

        return carry

    lax.fori_loop(0, chunks, settle_chunks, 0)
    save_text.wait()
    save_image.wait()


def solution(mesh):
    lanes = mesh.shape["lane"]
    planes = mesh.shape["block"] // 4
    cuts = 4

    def on_device(images, texts, labels):
        rows, width = images.shape
        share = rows // lanes
        parts = min(8, share // 16)
        pieces = min(4, share // 16)
        chunks = 2 * lanes
        dma = lambda n: pltpu.SemaphoreType.DMA((n,))
        hbm = pl.BlockSpec(memory_space=pltpu.HBM)
        free = pl.BlockSpec(memory_space=pl.ANY)
        half = lambda *s: pltpu.VMEM(s, BF16)
        full = lambda *s: pltpu.VMEM(s, F32)
        return pl.pallas_call(
            functools.partial(kernel, planes, lanes, parts, pieces, cuts),
            out_shape=(
                jax.ShapeDtypeStruct((share, width), F32),
                jax.ShapeDtypeStruct((share, width), F32),
            ),
            in_specs=[hbm, hbm, hbm],
            out_specs=(free, free),
            scratch_shapes=[
                half(4 * rows, width),
                half(planes, share, width),
                pltpu.VMEM((4, 1, rows), jnp.int32),
                full(4 * rows, width),
                full(planes, share, width),
                half(planes, share, width),
                half(planes, share, width),
                half(planes, share, width),
                half(2, rows, width),
                half(2, rows, width),
                half(rows, width),
                half(rows, width),
                half(3 * lanes, share // 2, width),
                half(3 * lanes, share // 2, width),
                full(share, width),
                dma(3), dma(1), dma(1), dma(pieces), *[dma(lanes * pieces)] * 4,
                dma(3), dma(3), *[dma(cuts * planes)] * 3,
                dma(planes * parts), dma(planes * parts), dma(planes * parts),
                dma(2 * chunks), dma(2 * chunks), dma(chunks), dma(chunks), dma(3 * lanes), dma(3 * lanes),
            ],
            compiler_params=pltpu.CompilerParams(
                collective_id=0, has_side_effects=True, vmem_limit_bytes=50 * 1024 * 1024
            ),
        )(images, texts, labels.reshape(1, rows))

    return jax.shard_map(
        on_device,
        mesh=mesh,
        in_specs=(P("block", None), P("block", None), P("block")),
        out_specs=(P(("block", "lane"), None), P(("block", "lane"), None)),
        check_vma=False,
    )
```

```python
import functools

import jax
import jax.numpy as jnp
from jax import lax
from jax.experimental import pallas as pl
from jax.experimental.pallas import tpu as pltpu
from jax.sharding import PartitionSpec as P

logit_bias = -6.0
MESH = pl.DeviceIdType.MESH
F32 = jnp.float32
BF16 = jnp.bfloat16


def kernel(
    planes, lanes, parts, pieces, cuts,
    images, texts, labels, image_out, text_out,
    img, txt, lab, acc, own, above, below, passing, c_out, c_in, x_out, x_in, y_out, y_in, kept,
    local_sem, i_send, i_recv, fx_send, fy_send, fc_send, f_recv, n_recv,
    l_send, l_recv, t_up, t_down, t_recv,
    g_send, a_recv, b_recv, c_send, c_recv, x_send, x_recv, y_send, y_recv,
):
    rows = images.shape[0]
    share = rows // lanes
    cut = share // cuts
    fine = share // pieces
    part = share // parts
    chunks = 2 * lanes
    tall = rows // chunks
    block = lax.axis_index("block")
    y = lax.axis_index("lane")
    p, x, c = block // 4, (block // 2) % 2, block % 2

    def at(plane, xx, cc, lane=None):
        return {"block": plane * 4 + xx * 2 + cc, "lane": y if lane is None else lane}

    def remote(src, dst, send, recv, device):
        return pltpu.make_async_remote_copy(
            src_ref=src, dst_ref=dst, send_sem=send, recv_sem=recv, device_id=device, device_id_type=MESH
        )

    other_core, other_x, corner = at(p, x, 1 - c), at(p, 1 - x, c), at(p, 1 - x, 1 - c)
    has_up, has_down = p < planes - 1, p > 0
    up, down = at(p + 1, x, c), at(p - 1, x, c)

    def block_rows(index):
        return pl.ds(pl.multiple_of(index * rows, rows), rows)

    mine = x * 2 + c
    far = (1 - x) * 2 + c

    barrier = pltpu.get_barrier_semaphore()

    def greet(device):
        pl.semaphore_signal(barrier, inc=1, device_id=device, device_id_type=MESH)

    greet(other_core)
    greet(other_x)
    greet(corner)
    for step in range(1, lanes):
        greet(at(p, x, c, lax.rem(y + step, lanes)))

    @pl.when(has_up)
    def _():
        greet(up)

    @pl.when(has_down)
    def _():
        greet(down)

    load_txt = pltpu.make_async_copy(
        texts.at[pl.ds(pl.multiple_of(y * share, share), share)], own.at[0], local_sem.at[1]
    )
    load_img = pltpu.make_async_copy(images, acc.at[pl.ds(0, rows)], local_sem.at[0])
    keep_lab = pltpu.make_async_copy(labels, lab.at[mine], local_sem.at[2])
    load_txt.start()
    load_img.start()
    keep_lab.start()
    load_txt.wait()
    txt[p] = own[0].astype(BF16)
    pl.semaphore_wait(barrier, 2 + lanes + has_up.astype(jnp.int32) + has_down.astype(jnp.int32))

    def text_copy(q, half, going_up):
        spot = txt.at[q, pl.ds(pl.multiple_of(half * cut, cut), cut)]
        index = q * cuts + half
        return remote(
            spot, spot, (t_up if going_up else t_down).at[index], t_recv.at[index], up if going_up else down
        )

    @pl.when(has_up)
    def _():
        for half in range(cuts):
            text_copy(p, half, True).start()

    @pl.when(has_down)
    def _():
        for half in range(cuts):
            text_copy(p, half, False).start()

    def text_passes(t, half):
        low, high = p - t, p + t

        @pl.when((low >= 0) & has_up)
        def _():
            text_copy(low, half, True).wait_recv()
            text_copy(low, half, True).start()

        @pl.when((high < planes) & has_down)
        def _():
            text_copy(high, half, False).wait_recv()
            text_copy(high, half, False).start()

    def text_stays(t, half):
        low, high = p - t, p + t

        @pl.when((low >= 0) & jnp.logical_not(has_up))
        def _():
            text_copy(low, half, True).wait_recv()

        @pl.when((high < planes) & jnp.logical_not(has_down))
        def _():
            text_copy(high, half, False).wait_recv()

    image_near = remote(img.at[block_rows(mine)], img.at[block_rows(mine)], i_send.at[0], i_recv.at[0], other_core)

    def piece_rows(index, lane, piece):
        return pl.ds(pl.multiple_of(index * rows + lane * share + piece * fine, fine), fine)

    def far_x(piece):
        spot = img.at[piece_rows(mine, y, piece)]
        return remote(
            spot, spot, fx_send.at[piece], f_recv.at[y * pieces + piece], other_x
        )

    def far_y(step, piece):
        spot = img.at[piece_rows(far, y, piece)]
        device = at(p, x, c, lax.rem(y + step, lanes))
        return remote(spot, spot, fy_send.at[step * pieces + piece], f_recv.at[y * pieces + piece], device)

    def far_core(lane, piece):
        spot = img.at[piece_rows(far, lane, piece)]
        return remote(spot, spot, fc_send.at[lane * pieces + piece], n_recv.at[lane * pieces + piece], other_core)

    def far_arrived(lane, piece):
        spot = img.at[piece_rows(far, lane, piece)]
        return remote(spot, spot, fx_send.at[piece], f_recv.at[lane * pieces + piece], other_x)
    label_copies = [
        remote(labels, lab.at[mine], l_send.at[k], l_recv.at[k], device)
        for k, device in enumerate((other_core, other_x, corner))
    ]
    for copy in label_copies:
        copy.start()
    load_img.wait()
    img[block_rows(mine)] = acc[pl.ds(0, rows)].astype(BF16)
    for piece in range(pieces):
        far_x(piece).start()
    image_near.start()
    acc[...] = jnp.zeros_like(acc)
    own[...] = jnp.zeros_like(own)
    keep_lab.wait()
    for copy in label_copies:
        copy.wait_recv()
    image_near.wait_recv()

    def tile(q, index, start, height):
        spot = (q, pl.ds(pl.multiple_of(start, height), height))
        text_now = txt[spot]
        first = (q * 4 + x * 2 + c) * rows + y * share + start
        text_ids = first + lax.broadcasted_iota(jnp.int32, (height, rows), 0)
        image_now = img[block_rows(index)]
        logits = lax.dot_general(
            text_now, image_now, (((1,), (1,)), ((), ())), preferred_element_type=F32
        ) + logit_bias
        positive = (lab[index] == text_ids).astype(F32)
        weights = (jax.nn.sigmoid(logits) - positive).astype(BF16)
        own[spot] += jnp.dot(weights, image_now, preferred_element_type=F32)
        acc[block_rows(index)] += lax.dot_general(
            weights, text_now, (((0,), (0,)), ((), ())), preferred_element_type=F32
        )

    def compute(q, xx):
        for cc in range(2):
            tile(q, xx * 2 + cc, 0, share)

    def pass_to_core(piece):
        for step in range(1, lanes):
            lane = lax.rem(y + step, lanes)
            far_arrived(lane, piece).wait_recv()
            far_core(lane, piece).start()

    def gather(piece, carry):
        far_arrived(y, piece).wait_recv()
        for step in range(1, lanes):
            far_y(step, piece).start()
        far_core(y, piece).start()

        def text_pieces(half, carry):
            text_passes(1, half)
            text_stays(1, half)
            return carry

        lax.fori_loop(piece * cuts // pieces, (piece + 1) * cuts // pieces, text_pieces, 0)

        @pl.when(piece == 0)
        def _():
            compute(p, x)

        return carry

    lax.fori_loop(0, pieces, gather, 0)

    last_compute = jnp.maximum(p, planes - 1 - p)

    def grad_copy(q, k, going_up):
        spot = (q, pl.ds(pl.multiple_of(k * part, part), part))
        index = q * parts + k
        return remote(
            passing.at[spot], (below if going_up else above).at[spot], g_send.at[index],
            (b_recv if going_up else a_recv).at[index], up if going_up else down,
        )

    def chunk_rows(m):
        return pl.ds(pl.multiple_of(m * tall, tall), tall)

    def c_copy(xx, m):
        index = xx * chunks + m
        return remote(
            c_out.at[xx, chunk_rows(m)], c_in.at[xx, chunk_rows(m)], c_send.at[index], c_recv.at[index], other_core
        )

    def x_copy(m):
        index = jnp.int32(m)
        return remote(
            x_out.at[chunk_rows(index)], x_in.at[chunk_rows(index)], x_send.at[index], x_recv.at[index], other_x
        )

    def y_copy(lane, kind):
        slot = lax.rem(lane - y + lanes, lanes)
        index = slot * 3 + kind
        return remote(y_out.at[index], y_in.at[index], y_send.at[index], y_recv.at[index], at(p, x, c, lane))

    def acc_rows(index, m):
        return pl.ds(pl.multiple_of(index * rows + m * tall, tall), tall)

    toward = jnp.where(2 * p < planes, 1, -1)
    own_step = min(2, planes - 1)
    far_item = 3 if planes > 2 else 0
    ends_last = last_compute == planes - 1
    lag = 3
    early = parts * 5 // 8
    first_parts = parts * 5 // 8 if planes > 3 else parts
    at_first_hop = last_compute * (parts + lag) + jnp.where(ends_last, 0, 1)
    at_second_hop = jnp.where(ends_last, last_compute, last_compute + 1) * (parts + lag) + jnp.where(ends_last, 0, 3)

    def one_step(t, carry):
        apart = ends_last & (t == planes - 1)

        def one_item(i, carry):
            q = jnp.where(i == 0, p, jnp.where(i % 2 == 1, p + toward * t, p - toward * t))
            xx = jnp.where((i == 1) | (i == 2), x, 1 - x)
            valid = jnp.where(i == 0, t == own_step, (q >= 0) & (q < planes) & jnp.logical_not(apart))

            @pl.when((t == 1) & (i == min(2, far_item)))
            def _():
                for piece in range(pieces):
                    pass_to_core(piece)

            @pl.when((t == 1) & (i == far_item))
            def _():
                for piece in range(pieces):
                    for step in range(lanes):
                        far_core(lax.rem(y + step, lanes), piece).wait_recv()

            @pl.when((t > 1) & (i == 1) & jnp.logical_not(apart))
            def _():
                for half in range(cuts):
                    text_stays(t, half)

            @pl.when(valid)
            def _():
                compute(q, xx)

            @pl.when(i > 0)
            def _():
                def pass_on(half, carry):
                    text_passes(t + 1, half)
                    return carry

                lax.fori_loop((i - 1) * cuts // 4, i * cuts // 4, pass_on, 0)

            return carry

        lax.fori_loop(0, 5, one_item, 0)

        def send_to_core():
            def send(n, carry):
                half, xx = n // (2 * lanes), jnp.where((n // lanes) % 2 == 0, 1 - x, x)
                m = lax.rem(y + 1 + n, lanes) * 2 + half
                c_out[xx, chunk_rows(m)] = acc[acc_rows(xx * 2 + 1 - c, m)].astype(BF16)
                c_copy(xx, m).start()
                return carry

            lax.fori_loop(0, 4 * lanes, send, 0)

        @pl.when((t == last_compute) & jnp.logical_not(ends_last))
        def _():
            send_to_core()

        def second_half(lane, xx):
            m = lane * 2

            @pl.when(lane != y)
            def _():
                c_copy(xx, m + 1).wait_recv()
                y_out[lax.rem(lane - y + lanes, lanes) * 3 + 1 + xx] = (
                    acc[acc_rows(xx * 2 + c, m + 1)] + c_in[xx, chunk_rows(m + 1)].astype(F32)
                ).astype(BF16)
                y_copy(lane, 1 + xx).start()

        def first_hop(n, carry):
            lane = lax.rem(y + 1 + n, lanes)
            m = lane * 2
            c_copy(1 - x, m).wait_recv()
            x_out[chunk_rows(m)] = (
                acc[acc_rows(far, m)] + c_in[1 - x, chunk_rows(m)].astype(F32)
            ).astype(BF16)
            x_copy(m).start()

            second_half(lane, 1 - x)
            return carry

        def first_hop_near(n, carry):
            second_half(lax.rem(y + 1 + n, lanes), x)
            return carry

        def second_hop(n, carry):
            lane = lax.rem(y + 1 + n, lanes)
            m = lane * 2
            c_copy(x, m).wait_recv()
            x_copy(m).wait_recv()
            total = (
                acc[acc_rows(mine, m)] + c_in[x, chunk_rows(m)].astype(F32) + x_in[chunk_rows(m)].astype(F32)
            )

            @pl.when(lane == y)
            def _():
                kept[pl.ds(0, tall)] = total

            @pl.when(lane != y)
            def _():
                y_out[lax.rem(lane - y + lanes, lanes) * 3] = total.astype(BF16)
                y_copy(lane, 0).start()

            return carry

        def gathered(xx):
            m = y * 2 + 1
            c_copy(xx, m).wait_recv()
            total = acc[acc_rows(xx * 2 + c, m)] + c_in[xx, chunk_rows(m)].astype(F32)
            for step in range(1, lanes):
                y_copy(lax.rem(y + step, lanes), 1 + xx).wait_recv()
                total = total + y_in[step * 3 + 1 + xx].astype(F32)
            return total

        def send_last():
            x_out[chunk_rows(1)] = gathered(1 - x).astype(BF16)
            x_copy(1).start()

        def grad_start(q, going_up, first, last):
            def one_part(k, carry):
                spot = (q, pl.ds(pl.multiple_of(k * part, part), part))
                passing[spot] = own[spot].astype(BF16)
                grad_copy(q, k, going_up).start()
                return carry

            lax.fori_loop(first, last, one_part, 0)

        def grad_starts(t, first, last):
            @pl.when(p == 0)
            def _():
                grad_start(t, True, first, last)

            @pl.when(p == planes - 1)
            def _():
                grad_start(planes - 1 - t, False, first, last)

        @pl.when(ends_last & (t < planes - 1))
        def _():
            grad_starts(t, 0, jnp.where(t == 1, early, jnp.where(t == planes - 2, first_parts, parts)))

        @pl.when(apart)
        def _():
            def one_slice(h, carry):
                def arrive(half, carry):
                    text_stays(t, half)
                    return carry

                lax.fori_loop(h * cuts // 2, (h + 1) * cuts // 2, arrive, 0)

                def one_tile(n, carry):
                    index = jnp.where(n % 2 == 0, 1 - x, x) * 2 + jnp.where(n < 2, 1 - c, c)
                    tile(p + toward * t, index, h * (share // 2), share // 2)

                    @pl.when((h == 1) & (n == 1))
                    def _():
                        send_to_core()

                    @pl.when((h == 1) & (n == 2))
                    def _():
                        lax.fori_loop(0, lanes, first_hop, 0)

                    @pl.when((h == 1) & (n == 3))
                    def _():
                        lax.fori_loop(0, lanes, first_hop_near, 0)

                    return carry

                lax.fori_loop(0, 4, one_tile, 0)
                grad_starts(t, h * parts // 2, (h + 1) * parts // 2)
                return carry

            lax.fori_loop(0, 2, one_slice, 0)
            grad_starts(jnp.int32(planes - 2), first_parts, parts)
            grad_starts(jnp.int32(1), early, parts)

        def pass_grads(t, k_up, k_down, goes):
            def spot_of(q, k):
                return (q, pl.ds(pl.multiple_of(k * part, part), part))

            @pl.when((t > p) & has_down & (k_up >= 0) & (k_up < goes))
            def _():
                spot = spot_of(t, k_up)
                grad_copy(t, k_up, True).wait_recv()
                passing[spot] = (own[spot] + below[spot].astype(F32)).astype(BF16)
                grad_copy(t, k_up, True).start()

            q_above = planes - 1 - t

            @pl.when((q_above < p) & has_up & (k_down >= 0) & (k_down < goes))
            def _():
                spot = spot_of(q_above, k_down)
                grad_copy(q_above, k_down, False).wait_recv()
                passing[spot] = (own[spot] + above[spot].astype(F32)).astype(BF16)
                grad_copy(q_above, k_down, False).start()

        def one_part(k, carry):
            at_now = t * (parts + lag) + k
            k_up = k - jnp.where(2 * p < planes, 0, lag)
            k_down = k - jnp.where(2 * p < planes, lag, 0)

            @pl.when((at_now == at_first_hop) & jnp.logical_not(ends_last))
            def _():
                lax.fori_loop(0, lanes, first_hop, 0)
                lax.fori_loop(0, lanes, first_hop_near, 0)

            @pl.when(at_now == at_second_hop)
            def _():
                lax.fori_loop(0, lanes - 1, second_hop, 0)
                send_last()

            goes = jnp.where(t == planes - 2, first_parts, parts)
            pass_grads(t, k_up, k_down, goes)
            return carry

        lax.fori_loop(0, parts + lag, one_part, 0)

        @pl.when(t == planes - 1)
        def _():
            def late_part(k, carry):
                pass_grads(planes - 2, k, k, parts)
                return carry

            lax.fori_loop(first_parts, parts, late_part, 0)
            lax.fori_loop(lanes - 1, lanes, second_hop, 0)
            kept[pl.ds(tall, tall)] = gathered(x)

        return carry

    lax.fori_loop(1, planes, one_step, 0)

    for piece in range(pieces):
        far_x(piece).wait_send()
        for step in range(lanes):
            far_core(lax.rem(y + step, lanes), piece).wait_send()
            if step > 0:
                far_y(step, piece).wait_send()
    image_near.wait_send()
    for copy in label_copies:
        copy.wait_send()

    def settle(q, carry):
        @pl.when((q <= p) & has_up)
        def _():
            for half in range(cuts):
                text_copy(q, half, True).wait_send()

        @pl.when((q >= p) & has_down)
        def _():
            for half in range(cuts):
                text_copy(q, half, False).wait_send()

        return carry

    lax.fori_loop(0, planes, settle, 0)

    def last_sums(k, carry):
        spot = (p, pl.ds(pl.multiple_of(k * part, part), part))

        @pl.when(has_up)
        def _():
            grad_copy(p, k, False).wait_recv()
            own[spot] += above[spot].astype(F32)

        @pl.when(has_down)
        def _():
            grad_copy(p, k, True).wait_recv()
            own[spot] += below[spot].astype(F32)

        return carry

    lax.fori_loop(0, parts, last_sums, 0)
    save_text = pltpu.make_async_copy(own.at[p], text_out, local_sem.at[1])
    save_text.start()
    first_half = kept[pl.ds(0, tall)]
    for step in range(1, lanes):
        y_copy(lax.rem(y + step, lanes), 0).wait_recv()
        first_half = first_half + y_in[step * 3].astype(F32)
    kept[pl.ds(0, tall)] = first_half
    x_copy(1).wait_recv()
    kept[pl.ds(tall, tall)] += x_in[chunk_rows(1)].astype(F32)
    save_image = pltpu.make_async_copy(kept, image_out, local_sem.at[0])
    save_image.start()
    for step in range(1, lanes):
        for kind in range(3):
            y_copy(lax.rem(y + step, lanes), kind).wait_send()
    x_copy(1).wait_send()

    def settle_grads(q, carry):
        @pl.when(q != p)
        def _():
            def one_part(k, carry):
                grad_copy(q, k, True).wait_send()
                return carry

            lax.fori_loop(0, parts, one_part, 0)

        return carry

    lax.fori_loop(0, planes, settle_grads, 0)

    def settle_chunks(m, carry):
        c_copy(0, m).wait_send()
        c_copy(1, m).wait_send()

        @pl.when(m % 2 == 0)
        def _():
            x_copy(m).wait_send()

        return carry

    lax.fori_loop(0, chunks, settle_chunks, 0)
    save_text.wait()
    save_image.wait()


def solution(mesh):
    lanes = mesh.shape["lane"]
    planes = mesh.shape["block"] // 4
    cuts = 4

    def on_device(images, texts, labels):
        rows, width = images.shape
        share = rows // lanes
        parts = min(8, share // 16)
        pieces = min(8, share // 16)
        chunks = 2 * lanes
        dma = lambda n: pltpu.SemaphoreType.DMA((n,))
        hbm = pl.BlockSpec(memory_space=pltpu.HBM)
        free = pl.BlockSpec(memory_space=pl.ANY)
        half = lambda *s: pltpu.VMEM(s, BF16)
        full = lambda *s: pltpu.VMEM(s, F32)
        return pl.pallas_call(
            functools.partial(kernel, planes, lanes, parts, pieces, cuts),
            out_shape=(
                jax.ShapeDtypeStruct((share, width), F32),
                jax.ShapeDtypeStruct((share, width), F32),
            ),
            in_specs=[hbm, hbm, hbm],
            out_specs=(free, free),
            scratch_shapes=[
                half(4 * rows, width),
                half(planes, share, width),
                pltpu.VMEM((4, 1, rows), jnp.int32),
                full(4 * rows, width),
                full(planes, share, width),
                half(planes, share, width),
                half(planes, share, width),
                half(planes, share, width),
                half(2, rows, width),
                half(2, rows, width),
                half(rows, width),
                half(rows, width),
                half(3 * lanes, share // 2, width),
                half(3 * lanes, share // 2, width),
                full(share, width),
                dma(3), dma(1), dma(1), dma(pieces), *[dma(lanes * pieces)] * 4,
                dma(3), dma(3), *[dma(cuts * planes)] * 3,
                dma(planes * parts), dma(planes * parts), dma(planes * parts),
                dma(2 * chunks), dma(2 * chunks), dma(chunks), dma(chunks), dma(3 * lanes), dma(3 * lanes),
            ],
            compiler_params=pltpu.CompilerParams(
                collective_id=0, has_side_effects=True, vmem_limit_bytes=50 * 1024 * 1024
            ),
        )(images, texts, labels.reshape(1, rows))

    return jax.shard_map(
        on_device,
        mesh=mesh,
        in_specs=(P("block", None), P("block", None), P("block")),
        out_specs=(P(("block", "lane"), None), P(("block", "lane"), None)),
        check_vma=False,
    )
```

```python
import functools

import jax
import jax.numpy as jnp
from jax import lax
from jax.experimental import pallas as pl
from jax.experimental.pallas import tpu as pltpu
from jax.sharding import PartitionSpec as P

logit_bias = -6.0
MESH = pl.DeviceIdType.MESH
F32 = jnp.float32
BF16 = jnp.bfloat16


def kernel(
    planes, lanes, parts, pieces, cuts,
    images, texts, labels, image_out, text_out,
    img, txt, lab, acc, own, above, below, passing, c_out, c_in, x_out, x_in, y_out, y_in, kept,
    local_sem, i_send, i_recv, fx_send, fy_send, fc_send, f_recv, n_recv,
    l_send, l_recv, t_up, t_down, t_recv,
    g_send, a_recv, b_recv, c_send, c_recv, x_send, x_recv, y_send, y_recv,
):
    rows = images.shape[0]
    share = rows // lanes
    cut = share // cuts
    fine = share // pieces
    part = share // parts
    chunks = 2 * lanes
    tall = rows // chunks
    block = lax.axis_index("block")
    y = lax.axis_index("lane")
    p, x, c = block // 4, (block // 2) % 2, block % 2

    def at(plane, xx, cc, lane=None):
        return {"block": plane * 4 + xx * 2 + cc, "lane": y if lane is None else lane}

    def remote(src, dst, send, recv, device):
        return pltpu.make_async_remote_copy(
            src_ref=src, dst_ref=dst, send_sem=send, recv_sem=recv, device_id=device, device_id_type=MESH
        )

    other_core, other_x, corner = at(p, x, 1 - c), at(p, 1 - x, c), at(p, 1 - x, 1 - c)
    has_up, has_down = p < planes - 1, p > 0
    up, down = at(p + 1, x, c), at(p - 1, x, c)

    def block_rows(index):
        return pl.ds(pl.multiple_of(index * rows, rows), rows)

    mine = x * 2 + c
    far = (1 - x) * 2 + c

    barrier = pltpu.get_barrier_semaphore()

    def greet(device):
        pl.semaphore_signal(barrier, inc=1, device_id=device, device_id_type=MESH)

    greet(other_core)
    greet(other_x)
    greet(corner)
    for step in range(1, lanes):
        greet(at(p, x, c, lax.rem(y + step, lanes)))

    @pl.when(has_up)
    def _():
        greet(up)

    @pl.when(has_down)
    def _():
        greet(down)

    load_txt = pltpu.make_async_copy(
        texts.at[pl.ds(pl.multiple_of(y * share, share), share)], own.at[0], local_sem.at[1]
    )
    load_img = pltpu.make_async_copy(images, acc.at[pl.ds(0, rows)], local_sem.at[0])
    keep_lab = pltpu.make_async_copy(labels, lab.at[mine], local_sem.at[2])
    load_txt.start()
    load_img.start()
    keep_lab.start()
    load_txt.wait()
    txt[p] = own[0].astype(BF16)
    pl.semaphore_wait(barrier, 2 + lanes + has_up.astype(jnp.int32) + has_down.astype(jnp.int32))

    def text_copy(q, half, going_up):
        spot = txt.at[q, pl.ds(pl.multiple_of(half * cut, cut), cut)]
        index = q * cuts + half
        return remote(
            spot, spot, (t_up if going_up else t_down).at[index], t_recv.at[index], up if going_up else down
        )

    @pl.when(has_up)
    def _():
        for half in range(cuts):
            text_copy(p, half, True).start()

    @pl.when(has_down)
    def _():
        for half in range(cuts):
            text_copy(p, half, False).start()

    def text_passes(t, half):
        low, high = p - t, p + t

        @pl.when((low >= 0) & has_up)
        def _():
            text_copy(low, half, True).wait_recv()
            text_copy(low, half, True).start()

        @pl.when((high < planes) & has_down)
        def _():
            text_copy(high, half, False).wait_recv()
            text_copy(high, half, False).start()

    def text_stays(t, half):
        low, high = p - t, p + t

        @pl.when((low >= 0) & jnp.logical_not(has_up))
        def _():
            text_copy(low, half, True).wait_recv()

        @pl.when((high < planes) & jnp.logical_not(has_down))
        def _():
            text_copy(high, half, False).wait_recv()

    image_near = remote(img.at[block_rows(mine)], img.at[block_rows(mine)], i_send.at[0], i_recv.at[0], other_core)

    def piece_rows(index, lane, piece):
        return pl.ds(pl.multiple_of(index * rows + lane * share + piece * fine, fine), fine)

    def far_x(piece):
        spot = img.at[piece_rows(mine, y, piece)]
        return remote(
            spot, spot, fx_send.at[piece], f_recv.at[y * pieces + piece], other_x
        )

    def far_y(step, piece):
        spot = img.at[piece_rows(far, y, piece)]
        device = at(p, x, c, lax.rem(y + step, lanes))
        return remote(spot, spot, fy_send.at[step * pieces + piece], f_recv.at[y * pieces + piece], device)

    def far_core(lane, piece):
        spot = img.at[piece_rows(far, lane, piece)]
        return remote(spot, spot, fc_send.at[lane * pieces + piece], n_recv.at[lane * pieces + piece], other_core)

    def far_arrived(lane, piece):
        spot = img.at[piece_rows(far, lane, piece)]
        return remote(spot, spot, fx_send.at[piece], f_recv.at[lane * pieces + piece], other_x)
    label_copies = [
        remote(labels, lab.at[mine], l_send.at[k], l_recv.at[k], device)
        for k, device in enumerate((other_core, other_x, corner))
    ]
    for copy in label_copies:
        copy.start()
    load_img.wait()
    first_rows = pl.ds(pl.multiple_of(y * share, share), share)
    img[pl.ds(pl.multiple_of(mine * rows + y * share, share), share)] = acc[first_rows].astype(BF16)
    for piece in range(pieces):
        far_x(piece).start()
    for step in range(1, lanes):
        lane = lax.rem(y + step, lanes)
        img[pl.ds(pl.multiple_of(mine * rows + lane * share, share), share)] = acc[
            pl.ds(pl.multiple_of(lane * share, share), share)
        ].astype(BF16)
    image_near.start()
    acc[...] = jnp.zeros_like(acc)
    own[...] = jnp.zeros_like(own)
    keep_lab.wait()
    for copy in label_copies:
        copy.wait_recv()
    image_near.wait_recv()

    def tile(q, index, start, height):
        spot = (q, pl.ds(pl.multiple_of(start, height), height))
        text_now = txt[spot]
        first = (q * 4 + x * 2 + c) * rows + y * share + start
        text_ids = first + lax.broadcasted_iota(jnp.int32, (height, rows), 0)
        image_now = img[block_rows(index)]
        logits = lax.dot_general(
            text_now, image_now, (((1,), (1,)), ((), ())), preferred_element_type=F32
        ) + logit_bias
        positive = (lab[index] == text_ids).astype(F32)
        weights = (jax.nn.sigmoid(logits) - positive).astype(BF16)
        own[spot] += jnp.dot(weights, image_now, preferred_element_type=F32)
        acc[block_rows(index)] += lax.dot_general(
            weights, text_now, (((0,), (0,)), ((), ())), preferred_element_type=F32
        )

    def compute(q, xx):
        for cc in range(2):
            tile(q, xx * 2 + cc, 0, share)

    def pass_to_core(piece):
        for step in range(1, lanes):
            lane = lax.rem(y + step, lanes)
            far_arrived(lane, piece).wait_recv()
            far_core(lane, piece).start()

    def gather(piece, carry):
        far_arrived(y, piece).wait_recv()
        for step in range(1, lanes):
            far_y(step, piece).start()
        far_core(y, piece).start()

        def text_pieces(half, carry):
            text_passes(1, half)
            text_stays(1, half)
            return carry

        lax.fori_loop(piece * cuts // pieces, (piece + 1) * cuts // pieces, text_pieces, 0)

        @pl.when(piece == 0)
        def _():
            compute(p, x)

        return carry

    lax.fori_loop(0, pieces, gather, 0)

    last_compute = jnp.maximum(p, planes - 1 - p)

    def grad_copy(q, k, going_up):
        spot = (q, pl.ds(pl.multiple_of(k * part, part), part))
        index = q * parts + k
        return remote(
            passing.at[spot], (below if going_up else above).at[spot], g_send.at[index],
            (b_recv if going_up else a_recv).at[index], up if going_up else down,
        )

    def chunk_rows(m):
        return pl.ds(pl.multiple_of(m * tall, tall), tall)

    def c_copy(xx, m):
        index = xx * chunks + m
        return remote(
            c_out.at[xx, chunk_rows(m)], c_in.at[xx, chunk_rows(m)], c_send.at[index], c_recv.at[index], other_core
        )

    def x_copy(m):
        index = jnp.int32(m)
        return remote(
            x_out.at[chunk_rows(index)], x_in.at[chunk_rows(index)], x_send.at[index], x_recv.at[index], other_x
        )

    def y_copy(lane, kind):
        slot = lax.rem(lane - y + lanes, lanes)
        index = slot * 3 + kind
        return remote(y_out.at[index], y_in.at[index], y_send.at[index], y_recv.at[index], at(p, x, c, lane))

    def acc_rows(index, m):
        return pl.ds(pl.multiple_of(index * rows + m * tall, tall), tall)

    toward = jnp.where(2 * p < planes, 1, -1)
    own_step = min(2, planes - 1)
    far_item = 3 if planes > 2 else 0
    ends_last = last_compute == planes - 1
    lag = 3
    early = parts * 5 // 8
    first_parts = parts * 5 // 8 if planes > 3 else parts
    at_first_hop = last_compute * (parts + lag) + jnp.where(ends_last, 0, 3)
    at_second_hop = jnp.where(ends_last, last_compute, last_compute + 1) * (parts + lag) + jnp.where(ends_last, 0, 3)

    def one_step(t, carry):
        apart = ends_last & (t == planes - 1)

        def one_item(i, carry):
            q = jnp.where(i == 0, p, jnp.where(i % 2 == 1, p + toward * t, p - toward * t))
            xx = jnp.where((i == 1) | (i == 2), x, 1 - x)
            valid = jnp.where(i == 0, t == own_step, (q >= 0) & (q < planes) & jnp.logical_not(apart))

            @pl.when((t == 1) & (i == min(2, far_item)))
            def _():
                for piece in range(pieces):
                    pass_to_core(piece)

            @pl.when((t == 1) & (i == far_item))
            def _():
                for piece in range(pieces):
                    for step in range(lanes):
                        far_core(lax.rem(y + step, lanes), piece).wait_recv()

            @pl.when((t > 1) & (i == 1) & jnp.logical_not(apart))
            def _():
                for half in range(cuts):
                    text_stays(t, half)

            @pl.when(valid)
            def _():
                compute(q, xx)

            @pl.when(i > 0)
            def _():
                def pass_on(half, carry):
                    text_passes(t + 1, half)
                    return carry

                lax.fori_loop((i - 1) * cuts // 4, i * cuts // 4, pass_on, 0)

            return carry

        lax.fori_loop(0, 5, one_item, 0)

        def send_to_core(xx):
            def send(n, carry):
                m = lax.rem(y + 1 + n, lanes) * 2 + n // lanes
                c_out[xx, chunk_rows(m)] = acc[acc_rows(xx * 2 + 1 - c, m)].astype(BF16)
                c_copy(xx, m).start()
                return carry

            lax.fori_loop(0, 2 * lanes, send, 0)

        @pl.when((t == last_compute) & jnp.logical_not(ends_last))
        def _():
            send_to_core(1 - x)
            send_to_core(x)

        def second_half(lane, xx):
            m = lane * 2

            @pl.when(lane != y)
            def _():
                c_copy(xx, m + 1).wait_recv()
                y_out[lax.rem(lane - y + lanes, lanes) * 3 + 1 + xx] = (
                    acc[acc_rows(xx * 2 + c, m + 1)] + c_in[xx, chunk_rows(m + 1)].astype(F32)
                ).astype(BF16)
                y_copy(lane, 1 + xx).start()

        def first_hop(n, carry):
            lane = lax.rem(y + 1 + n, lanes)
            m = lane * 2
            c_copy(1 - x, m).wait_recv()
            x_out[chunk_rows(m)] = (
                acc[acc_rows(far, m)] + c_in[1 - x, chunk_rows(m)].astype(F32)
            ).astype(BF16)
            x_copy(m).start()

            second_half(lane, 1 - x)
            return carry

        def first_hop_near(n, carry):
            second_half(lax.rem(y + 1 + n, lanes), x)
            return carry

        def second_hop(n, carry):
            lane = lax.rem(y + 1 + n, lanes)
            m = lane * 2
            c_copy(x, m).wait_recv()
            x_copy(m).wait_recv()
            total = (
                acc[acc_rows(mine, m)] + c_in[x, chunk_rows(m)].astype(F32) + x_in[chunk_rows(m)].astype(F32)
            )

            @pl.when(lane == y)
            def _():
                kept[pl.ds(0, tall)] = total

            @pl.when(lane != y)
            def _():
                y_out[lax.rem(lane - y + lanes, lanes) * 3] = total.astype(BF16)
                y_copy(lane, 0).start()

            return carry

        def gathered(xx):
            m = y * 2 + 1
            c_copy(xx, m).wait_recv()
            total = acc[acc_rows(xx * 2 + c, m)] + c_in[xx, chunk_rows(m)].astype(F32)
            for step in range(1, lanes):
                y_copy(lax.rem(y + step, lanes), 1 + xx).wait_recv()
                total = total + y_in[step * 3 + 1 + xx].astype(F32)
            return total

        def send_last():
            x_out[chunk_rows(1)] = gathered(1 - x).astype(BF16)
            x_copy(1).start()

        def grad_start(q, going_up, first, last):
            def one_part(k, carry):
                spot = (q, pl.ds(pl.multiple_of(k * part, part), part))
                passing[spot] = own[spot].astype(BF16)
                grad_copy(q, k, going_up).start()
                return carry

            lax.fori_loop(first, last, one_part, 0)

        def grad_starts(t, first, last):
            @pl.when(p == 0)
            def _():
                grad_start(t, True, first, last)

            @pl.when(p == planes - 1)
            def _():
                grad_start(planes - 1 - t, False, first, last)

        @pl.when(ends_last & (t < planes - 1))
        def _():
            grad_starts(t, 0, jnp.where(t == 1, early, jnp.where(t == planes - 2, first_parts, parts)))

        @pl.when(apart)
        def _():
            def one_slice(h, carry):
                def arrive(half, carry):
                    text_stays(t, half)
                    return carry

                lax.fori_loop(h * cuts // 2, (h + 1) * cuts // 2, arrive, 0)

                def one_tile(n, carry):
                    xx = jnp.where(n < 2, 1 - x, x)
                    index = xx * 2 + jnp.where(n % 2 == 0, 1 - c, c)
                    tile(p + toward * t, index, h * (share // 2), share // 2)

                    @pl.when((h == 1) & (n % 2 == 0))
                    def _():
                        send_to_core(xx)

                    @pl.when((h == 1) & (n == 1))
                    def _():
                        lax.fori_loop(0, lanes, first_hop, 0)

                    @pl.when((h == 1) & (n == 3))
                    def _():
                        lax.fori_loop(0, lanes, first_hop_near, 0)

                    return carry

                lax.fori_loop(0, 4, one_tile, 0)
                grad_starts(t, h * parts // 2, (h + 1) * parts // 2)
                return carry

            lax.fori_loop(0, 2, one_slice, 0)
            grad_starts(jnp.int32(planes - 2), first_parts, parts)
            grad_starts(jnp.int32(1), early, parts)

        def pass_grads(t, k_up, k_down, goes):
            def spot_of(q, k):
                return (q, pl.ds(pl.multiple_of(k * part, part), part))

            @pl.when((t > p) & has_down & (k_up >= 0) & (k_up < goes))
            def _():
                spot = spot_of(t, k_up)
                grad_copy(t, k_up, True).wait_recv()
                passing[spot] = (own[spot] + below[spot].astype(F32)).astype(BF16)
                grad_copy(t, k_up, True).start()

            q_above = planes - 1 - t

            @pl.when((q_above < p) & has_up & (k_down >= 0) & (k_down < goes))
            def _():
                spot = spot_of(q_above, k_down)
                grad_copy(q_above, k_down, False).wait_recv()
                passing[spot] = (own[spot] + above[spot].astype(F32)).astype(BF16)
                grad_copy(q_above, k_down, False).start()

        def one_part(k, carry):
            at_now = t * (parts + lag) + k
            k_up = k - jnp.where(2 * p < planes, 0, lag)
            k_down = k - jnp.where(2 * p < planes, lag, 0)

            @pl.when((at_now == at_first_hop) & jnp.logical_not(ends_last))
            def _():
                lax.fori_loop(0, lanes, first_hop, 0)
                lax.fori_loop(0, lanes, first_hop_near, 0)

            @pl.when(at_now == at_second_hop)
            def _():
                lax.fori_loop(0, lanes - 1, second_hop, 0)
                send_last()

            goes = jnp.where(t == planes - 2, first_parts, parts)
            pass_grads(t, k_up, k_down, goes)
            return carry

        lax.fori_loop(0, parts + lag, one_part, 0)

        @pl.when(t == planes - 1)
        def _():
            def late_part(k, carry):
                pass_grads(planes - 2, k, k, parts)
                return carry

            lax.fori_loop(first_parts, parts, late_part, 0)
            lax.fori_loop(lanes - 1, lanes, second_hop, 0)
            kept[pl.ds(tall, tall)] = gathered(x)

        return carry

    lax.fori_loop(1, planes, one_step, 0)

    for piece in range(pieces):
        far_x(piece).wait_send()
        for step in range(lanes):
            far_core(lax.rem(y + step, lanes), piece).wait_send()
            if step > 0:
                far_y(step, piece).wait_send()
    image_near.wait_send()
    for copy in label_copies:
        copy.wait_send()

    def settle(q, carry):
        @pl.when((q <= p) & has_up)
        def _():
            for half in range(cuts):
                text_copy(q, half, True).wait_send()

        @pl.when((q >= p) & has_down)
        def _():
            for half in range(cuts):
                text_copy(q, half, False).wait_send()

        return carry

    lax.fori_loop(0, planes, settle, 0)

    def last_sums(k, carry):
        spot = (p, pl.ds(pl.multiple_of(k * part, part), part))

        @pl.when(has_up)
        def _():
            grad_copy(p, k, False).wait_recv()
            own[spot] += above[spot].astype(F32)

        @pl.when(has_down)
        def _():
            grad_copy(p, k, True).wait_recv()
            own[spot] += below[spot].astype(F32)

        return carry

    lax.fori_loop(0, parts, last_sums, 0)
    save_text = pltpu.make_async_copy(own.at[p], text_out, local_sem.at[1])
    save_text.start()
    first_half = kept[pl.ds(0, tall)]
    for step in range(1, lanes):
        y_copy(lax.rem(y + step, lanes), 0).wait_recv()
        first_half = first_half + y_in[step * 3].astype(F32)
    kept[pl.ds(0, tall)] = first_half
    save_first = pltpu.make_async_copy(kept.at[pl.ds(0, tall)], image_out.at[pl.ds(0, tall)], local_sem.at[2])
    save_first.start()
    x_copy(1).wait_recv()
    kept[pl.ds(tall, tall)] += x_in[chunk_rows(1)].astype(F32)
    save_image = pltpu.make_async_copy(kept.at[pl.ds(tall, tall)], image_out.at[pl.ds(tall, tall)], local_sem.at[0])
    save_image.start()
    for step in range(1, lanes):
        for kind in range(3):
            y_copy(lax.rem(y + step, lanes), kind).wait_send()
    x_copy(1).wait_send()

    def settle_grads(q, carry):
        @pl.when(q != p)
        def _():
            def one_part(k, carry):
                grad_copy(q, k, True).wait_send()
                return carry

            lax.fori_loop(0, parts, one_part, 0)

        return carry

    lax.fori_loop(0, planes, settle_grads, 0)

    def settle_chunks(m, carry):
        c_copy(0, m).wait_send()
        c_copy(1, m).wait_send()

        @pl.when(m % 2 == 0)
        def _():
            x_copy(m).wait_send()

        return carry

    lax.fori_loop(0, chunks, settle_chunks, 0)
    save_text.wait()
    save_first.wait()
    save_image.wait()


def solution(mesh):
    lanes = mesh.shape["lane"]
    planes = mesh.shape["block"] // 4
    cuts = 4

    def on_device(images, texts, labels):
        rows, width = images.shape
        share = rows // lanes
        parts = min(8, share // 16)
        pieces = min(8, share // 16)
        chunks = 2 * lanes
        dma = lambda n: pltpu.SemaphoreType.DMA((n,))
        hbm = pl.BlockSpec(memory_space=pltpu.HBM)
        free = pl.BlockSpec(memory_space=pl.ANY)
        half = lambda *s: pltpu.VMEM(s, BF16)
        full = lambda *s: pltpu.VMEM(s, F32)
        return pl.pallas_call(
            functools.partial(kernel, planes, lanes, parts, pieces, cuts),
            out_shape=(
                jax.ShapeDtypeStruct((share, width), F32),
                jax.ShapeDtypeStruct((share, width), F32),
            ),
            in_specs=[hbm, hbm, hbm],
            out_specs=(free, free),
            scratch_shapes=[
                half(4 * rows, width),
                half(planes, share, width),
                pltpu.VMEM((4, 1, rows), jnp.int32),
                full(4 * rows, width),
                full(planes, share, width),
                half(planes, share, width),
                half(planes, share, width),
                half(planes, share, width),
                half(2, rows, width),
                half(2, rows, width),
                half(rows, width),
                half(rows, width),
                half(3 * lanes, share // 2, width),
                half(3 * lanes, share // 2, width),
                full(share, width),
                dma(3), dma(1), dma(1), dma(pieces), *[dma(lanes * pieces)] * 4,
                dma(3), dma(3), *[dma(cuts * planes)] * 3,
                dma(planes * parts), dma(planes * parts), dma(planes * parts),
                dma(2 * chunks), dma(2 * chunks), dma(chunks), dma(chunks), dma(3 * lanes), dma(3 * lanes),
            ],
            compiler_params=pltpu.CompilerParams(
                collective_id=0, has_side_effects=True, vmem_limit_bytes=50 * 1024 * 1024
            ),
        )(images, texts, labels.reshape(1, rows))

    return jax.shard_map(
        on_device,
        mesh=mesh,
        in_specs=(P("block", None), P("block", None), P("block")),
        out_specs=(P(("block", "lane"), None), P(("block", "lane"), None)),
        check_vma=False,
    )
```

```python
import functools

import jax
import jax.numpy as jnp
from jax import lax
from jax.experimental import pallas as pl
from jax.experimental.pallas import tpu as pltpu
from jax.sharding import PartitionSpec as P

logit_bias = -6.0
MESH = pl.DeviceIdType.MESH
F32 = jnp.float32
BF16 = jnp.bfloat16


def kernel(
    planes, lanes, parts, pieces, cuts,
    images, texts, labels, image_out, text_out,
    img, txt, lab, acc, own, above, below, passing, c_out, c_in, x_out, x_in, y_out, y_in, kept,
    local_sem, i_send, i_recv, fx_send, fy_send, fc_send, f_recv, n_recv,
    l_send, l_recv, t_up, t_down, t_recv,
    g_send, a_recv, b_recv, c_send, c_recv, x_send, x_recv, y_send, y_recv, s_sem,
):
    rows = images.shape[0]
    share = rows // lanes
    cut = share // cuts
    fine = share // pieces
    part = share // parts
    chunks = 2 * lanes
    tall = rows // chunks
    block = lax.axis_index("block")
    y = lax.axis_index("lane")
    p, x, c = block // 4, (block // 2) % 2, block % 2

    def at(plane, xx, cc, lane=None):
        return {"block": plane * 4 + xx * 2 + cc, "lane": y if lane is None else lane}

    def remote(src, dst, send, recv, device):
        return pltpu.make_async_remote_copy(
            src_ref=src, dst_ref=dst, send_sem=send, recv_sem=recv, device_id=device, device_id_type=MESH
        )

    other_core, other_x, corner = at(p, x, 1 - c), at(p, 1 - x, c), at(p, 1 - x, 1 - c)
    has_up, has_down = p < planes - 1, p > 0
    up, down = at(p + 1, x, c), at(p - 1, x, c)

    def block_rows(index):
        return pl.ds(pl.multiple_of(index * rows, rows), rows)

    mine = x * 2 + c
    far = (1 - x) * 2 + c

    barrier = pltpu.get_barrier_semaphore()

    def greet(device):
        pl.semaphore_signal(barrier, inc=1, device_id=device, device_id_type=MESH)

    greet(other_core)
    greet(other_x)
    greet(corner)
    for step in range(1, lanes):
        greet(at(p, x, c, lax.rem(y + step, lanes)))

    @pl.when(has_up)
    def _():
        greet(up)

    @pl.when(has_down)
    def _():
        greet(down)

    load_txt = pltpu.make_async_copy(
        texts.at[pl.ds(pl.multiple_of(y * share, share), share)], own.at[0], local_sem.at[1]
    )
    load_img = pltpu.make_async_copy(images, acc.at[pl.ds(0, rows)], local_sem.at[0])
    keep_lab = pltpu.make_async_copy(labels, lab.at[mine], local_sem.at[2])
    load_txt.start()
    load_img.start()
    keep_lab.start()
    load_txt.wait()
    txt[p] = own[0].astype(BF16)
    pl.semaphore_wait(barrier, 2 + lanes + has_up.astype(jnp.int32) + has_down.astype(jnp.int32))

    def text_copy(q, half, going_up):
        spot = txt.at[q, pl.ds(pl.multiple_of(half * cut, cut), cut)]
        index = q * cuts + half
        return remote(
            spot, spot, (t_up if going_up else t_down).at[index], t_recv.at[index], up if going_up else down
        )

    @pl.when(has_up)
    def _():
        for half in range(cuts):
            text_copy(p, half, True).start()

    @pl.when(has_down)
    def _():
        for half in range(cuts):
            text_copy(p, half, False).start()

    def text_passes(t, half):
        low, high = p - t, p + t

        @pl.when((low >= 0) & has_up)
        def _():
            text_copy(low, half, True).wait_recv()
            text_copy(low, half, True).start()

        @pl.when((high < planes) & has_down)
        def _():
            text_copy(high, half, False).wait_recv()
            text_copy(high, half, False).start()

    def text_stays(t, half):
        low, high = p - t, p + t

        @pl.when((low >= 0) & jnp.logical_not(has_up))
        def _():
            text_copy(low, half, True).wait_recv()

        @pl.when((high < planes) & jnp.logical_not(has_down))
        def _():
            text_copy(high, half, False).wait_recv()

    image_near = remote(img.at[block_rows(mine)], img.at[block_rows(mine)], i_send.at[0], i_recv.at[0], other_core)

    def piece_rows(index, lane, piece):
        return pl.ds(pl.multiple_of(index * rows + lane * share + piece * fine, fine), fine)

    def far_x(piece):
        spot = img.at[piece_rows(mine, y, piece)]
        return remote(
            spot, spot, fx_send.at[piece], f_recv.at[y * pieces + piece], other_x
        )

    def far_y(step, piece):
        spot = img.at[piece_rows(far, y, piece)]
        device = at(p, x, c, lax.rem(y + step, lanes))
        return remote(spot, spot, fy_send.at[step * pieces + piece], f_recv.at[y * pieces + piece], device)

    def far_core(lane, piece):
        spot = img.at[piece_rows(far, lane, piece)]
        return remote(spot, spot, fc_send.at[lane * pieces + piece], n_recv.at[lane * pieces + piece], other_core)

    def far_arrived(lane, piece):
        spot = img.at[piece_rows(far, lane, piece)]
        return remote(spot, spot, fx_send.at[piece], f_recv.at[lane * pieces + piece], other_x)
    label_copies = [
        remote(labels, lab.at[mine], l_send.at[k], l_recv.at[k], device)
        for k, device in enumerate((other_core, other_x, corner))
    ]
    for copy in label_copies:
        copy.start()
    load_img.wait()
    first_rows = pl.ds(pl.multiple_of(y * share, share), share)
    img[pl.ds(pl.multiple_of(mine * rows + y * share, share), share)] = acc[first_rows].astype(BF16)
    for piece in range(pieces):
        far_x(piece).start()
    for step in range(1, lanes):
        lane = lax.rem(y + step, lanes)
        img[pl.ds(pl.multiple_of(mine * rows + lane * share, share), share)] = acc[
            pl.ds(pl.multiple_of(lane * share, share), share)
        ].astype(BF16)
    image_near.start()
    acc[...] = jnp.zeros_like(acc)
    own[...] = jnp.zeros_like(own)
    keep_lab.wait()
    for copy in label_copies:
        copy.wait_recv()
    image_near.wait_recv()

    def tile(q, index, start, height):
        spot = (q, pl.ds(pl.multiple_of(start, height), height))
        text_now = txt[spot]
        first = (q * 4 + x * 2 + c) * rows + y * share + start
        text_ids = first + lax.broadcasted_iota(jnp.int32, (height, rows), 0)
        image_now = img[block_rows(index)]
        logits = lax.dot_general(
            text_now, image_now, (((1,), (1,)), ((), ())), preferred_element_type=F32
        ) + logit_bias
        positive = (lab[index] == text_ids).astype(F32)
        weights = (jax.nn.sigmoid(logits) - positive).astype(BF16)
        own[spot] += jnp.dot(weights, image_now, preferred_element_type=F32)
        acc[block_rows(index)] += lax.dot_general(
            weights, text_now, (((0,), (0,)), ((), ())), preferred_element_type=F32
        )

    def compute(q, xx):
        for cc in range(2):
            tile(q, xx * 2 + cc, 0, share)

    def pass_to_core(piece):
        for step in range(1, lanes):
            lane = lax.rem(y + step, lanes)
            far_arrived(lane, piece).wait_recv()
            far_core(lane, piece).start()

    def gather(piece, carry):
        far_arrived(y, piece).wait_recv()
        for step in range(1, lanes):
            far_y(step, piece).start()
        far_core(y, piece).start()

        def text_pieces(half, carry):
            text_passes(1, half)
            text_stays(1, half)
            return carry

        lax.fori_loop(piece * cuts // pieces, (piece + 1) * cuts // pieces, text_pieces, 0)

        @pl.when(piece == 0)
        def _():
            compute(p, x)

        return carry

    lax.fori_loop(0, pieces, gather, 0)

    last_compute = jnp.maximum(p, planes - 1 - p)

    def grad_copy(q, k, going_up):
        spot = (q, pl.ds(pl.multiple_of(k * part, part), part))
        index = q * parts + k
        return remote(
            passing.at[spot], (below if going_up else above).at[spot], g_send.at[index],
            (b_recv if going_up else a_recv).at[index], up if going_up else down,
        )

    def chunk_rows(m):
        return pl.ds(pl.multiple_of(m * tall, tall), tall)

    def c_copy(xx, m):
        index = xx * chunks + m
        return remote(
            c_out.at[xx, chunk_rows(m)], c_in.at[xx, chunk_rows(m)], c_send.at[index], c_recv.at[index], other_core
        )

    def x_copy(m):
        index = jnp.int32(m)
        return remote(
            x_out.at[chunk_rows(index)], x_in.at[chunk_rows(index)], x_send.at[index], x_recv.at[index], other_x
        )

    def y_copy(lane, kind):
        slot = lax.rem(lane - y + lanes, lanes)
        index = slot * 3 + kind
        return remote(y_out.at[index], y_in.at[index], y_send.at[index], y_recv.at[index], at(p, x, c, lane))

    def acc_rows(index, m):
        return pl.ds(pl.multiple_of(index * rows + m * tall, tall), tall)

    toward = jnp.where(2 * p < planes, 1, -1)
    own_step = min(2, planes - 1)
    far_item = 3 if planes > 2 else 0
    ends_last = last_compute == planes - 1
    lag = 3
    early = parts * 5 // 8
    first_parts = parts * 5 // 8 if planes > 3 else parts
    at_first_hop = last_compute * (parts + lag) + jnp.where(ends_last, 0, 3)
    at_second_hop = jnp.where(ends_last, last_compute, last_compute + 1) * (parts + lag) + jnp.where(ends_last, 0, 3)

    def one_step(t, carry):
        apart = ends_last & (t == planes - 1)

        def one_item(i, carry):
            q = jnp.where(i == 0, p, jnp.where(i % 2 == 1, p + toward * t, p - toward * t))
            xx = jnp.where((i == 1) | (i == 2), x, 1 - x)
            valid = jnp.where(i == 0, t == own_step, (q >= 0) & (q < planes) & jnp.logical_not(apart))

            @pl.when((t == 1) & (i == min(2, far_item)))
            def _():
                for piece in range(pieces):
                    pass_to_core(piece)

            @pl.when((t == 1) & (i == far_item))
            def _():
                for piece in range(pieces):
                    for step in range(lanes):
                        far_core(lax.rem(y + step, lanes), piece).wait_recv()

            @pl.when((t > 1) & (i == 1) & jnp.logical_not(apart))
            def _():
                for half in range(cuts):
                    text_stays(t, half)

            @pl.when(valid)
            def _():
                compute(q, xx)

            @pl.when(i > 0)
            def _():
                def pass_on(half, carry):
                    text_passes(t + 1, half)
                    return carry

                lax.fori_loop((i - 1) * cuts // 4, i * cuts // 4, pass_on, 0)

            return carry

        lax.fori_loop(0, 5, one_item, 0)

        def send_to_core(xx):
            def send(n, carry):
                m = lax.rem(y + 1 + n, lanes) * 2 + n // lanes
                c_out[xx, chunk_rows(m)] = acc[acc_rows(xx * 2 + 1 - c, m)].astype(BF16)
                c_copy(xx, m).start()
                return carry

            lax.fori_loop(0, 2 * lanes, send, 0)

        @pl.when((t == last_compute) & jnp.logical_not(ends_last))
        def _():
            send_to_core(1 - x)
            send_to_core(x)

        def second_half(lane, xx):
            m = lane * 2

            @pl.when(lane != y)
            def _():
                c_copy(xx, m + 1).wait_recv()
                y_out[lax.rem(lane - y + lanes, lanes) * 3 + 1 + xx] = (
                    acc[acc_rows(xx * 2 + c, m + 1)] + c_in[xx, chunk_rows(m + 1)].astype(F32)
                ).astype(BF16)
                y_copy(lane, 1 + xx).start()

        def first_hop(n, carry):
            lane = lax.rem(y + 1 + n, lanes)
            m = lane * 2
            c_copy(1 - x, m).wait_recv()
            x_out[chunk_rows(m)] = (
                acc[acc_rows(far, m)] + c_in[1 - x, chunk_rows(m)].astype(F32)
            ).astype(BF16)
            x_copy(m).start()

            second_half(lane, 1 - x)
            return carry

        def first_hop_near(n, carry):
            second_half(lax.rem(y + 1 + n, lanes), x)
            return carry

        def second_hop(n, carry):
            lane = lax.rem(y + 1 + n, lanes)
            m = lane * 2
            c_copy(x, m).wait_recv()
            x_copy(m).wait_recv()
            total = (
                acc[acc_rows(mine, m)] + c_in[x, chunk_rows(m)].astype(F32) + x_in[chunk_rows(m)].astype(F32)
            )

            @pl.when(lane == y)
            def _():
                kept[pl.ds(0, tall)] = total

            @pl.when(lane != y)
            def _():
                y_out[lax.rem(lane - y + lanes, lanes) * 3] = total.astype(BF16)
                y_copy(lane, 0).start()

            return carry

        def gathered(xx):
            m = y * 2 + 1
            c_copy(xx, m).wait_recv()
            total = acc[acc_rows(xx * 2 + c, m)] + c_in[xx, chunk_rows(m)].astype(F32)
            for step in range(1, lanes):
                y_copy(lax.rem(y + step, lanes), 1 + xx).wait_recv()
                total = total + y_in[step * 3 + 1 + xx].astype(F32)
            return total

        def send_last():
            x_out[chunk_rows(1)] = gathered(1 - x).astype(BF16)
            x_copy(1).start()

        def grad_start(q, going_up, first, last):
            def one_part(k, carry):
                spot = (q, pl.ds(pl.multiple_of(k * part, part), part))
                passing[spot] = own[spot].astype(BF16)
                grad_copy(q, k, going_up).start()
                return carry

            lax.fori_loop(first, last, one_part, 0)

        def grad_starts(t, first, last):
            @pl.when(p == 0)
            def _():
                grad_start(t, True, first, last)

            @pl.when(p == planes - 1)
            def _():
                grad_start(planes - 1 - t, False, first, last)

        @pl.when(ends_last & (t < planes - 1))
        def _():
            grad_starts(t, 0, jnp.where(t == 1, early, jnp.where(t == planes - 2, first_parts, parts)))

        @pl.when(apart)
        def _():
            def one_slice(h, carry):
                def arrive(half, carry):
                    text_stays(t, half)
                    return carry

                lax.fori_loop(h * cuts // 2, (h + 1) * cuts // 2, arrive, 0)

                def one_tile(n, carry):
                    xx = jnp.where(n < 2, 1 - x, x)
                    index = xx * 2 + jnp.where(n % 2 == 0, 1 - c, c)
                    tile(p + toward * t, index, h * (share // 2), share // 2)

                    @pl.when((h == 1) & (n % 2 == 0))
                    def _():
                        send_to_core(xx)

                    @pl.when((h == 1) & (n == 1))
                    def _():
                        lax.fori_loop(0, lanes, first_hop, 0)

                    @pl.when((h == 1) & (n == 3))
                    def _():
                        lax.fori_loop(0, lanes, first_hop_near, 0)

                    return carry

                lax.fori_loop(0, 4, one_tile, 0)
                grad_starts(t, h * parts // 2, (h + 1) * parts // 2)
                return carry

            lax.fori_loop(0, 2, one_slice, 0)
            grad_starts(jnp.int32(planes - 2), first_parts, parts)
            grad_starts(jnp.int32(1), early, parts)

        def pass_grads(t, k_up, k_down, goes):
            def spot_of(q, k):
                return (q, pl.ds(pl.multiple_of(k * part, part), part))

            @pl.when((t > p) & has_down & (k_up >= 0) & (k_up < goes))
            def _():
                spot = spot_of(t, k_up)
                grad_copy(t, k_up, True).wait_recv()
                passing[spot] = (own[spot] + below[spot].astype(F32)).astype(BF16)
                grad_copy(t, k_up, True).start()

            q_above = planes - 1 - t

            @pl.when((q_above < p) & has_up & (k_down >= 0) & (k_down < goes))
            def _():
                spot = spot_of(q_above, k_down)
                grad_copy(q_above, k_down, False).wait_recv()
                passing[spot] = (own[spot] + above[spot].astype(F32)).astype(BF16)
                grad_copy(q_above, k_down, False).start()

        def one_part(k, carry):
            at_now = t * (parts + lag) + k
            k_up = k - jnp.where(2 * p < planes, 0, lag)
            k_down = k - jnp.where(2 * p < planes, lag, 0)

            @pl.when((at_now == at_first_hop) & jnp.logical_not(ends_last))
            def _():
                lax.fori_loop(0, lanes, first_hop, 0)
                lax.fori_loop(0, lanes, first_hop_near, 0)

            @pl.when(at_now == at_second_hop)
            def _():
                lax.fori_loop(0, lanes - 1, second_hop, 0)
                send_last()

            goes = jnp.where(t == planes - 2, first_parts, parts)
            pass_grads(t, k_up, k_down, goes)
            return carry

        lax.fori_loop(0, parts + lag, one_part, 0)

        @pl.when(t == planes - 1)
        def _():
            def late_part(k, carry):
                pass_grads(planes - 2, k, k, parts)
                return carry

            lax.fori_loop(first_parts, parts, late_part, 0)
            lax.fori_loop(lanes - 1, lanes, second_hop, 0)
            kept[pl.ds(tall, tall)] = gathered(x)

        return carry

    lax.fori_loop(1, planes, one_step, 0)

    for piece in range(pieces):
        far_x(piece).wait_send()
        for step in range(lanes):
            far_core(lax.rem(y + step, lanes), piece).wait_send()
            if step > 0:
                far_y(step, piece).wait_send()
    image_near.wait_send()
    for copy in label_copies:
        copy.wait_send()

    def settle(q, carry):
        @pl.when((q <= p) & has_up)
        def _():
            for half in range(cuts):
                text_copy(q, half, True).wait_send()

        @pl.when((q >= p) & has_down)
        def _():
            for half in range(cuts):
                text_copy(q, half, False).wait_send()

        return carry

    lax.fori_loop(0, planes, settle, 0)

    def save_text(k):
        spot = pl.ds(pl.multiple_of(k * part, part), part)
        return pltpu.make_async_copy(own.at[p, spot], text_out.at[spot], s_sem.at[k])

    def last_sums(k, carry):
        spot = (p, pl.ds(pl.multiple_of(k * part, part), part))

        @pl.when(has_up)
        def _():
            grad_copy(p, k, False).wait_recv()
            own[spot] += above[spot].astype(F32)

        @pl.when(has_down)
        def _():
            grad_copy(p, k, True).wait_recv()
            own[spot] += below[spot].astype(F32)

        save_text(k).start()
        return carry

    lax.fori_loop(0, parts, last_sums, 0)
    first_half = kept[pl.ds(0, tall)]
    for step in range(1, lanes):
        y_copy(lax.rem(y + step, lanes), 0).wait_recv()
        first_half = first_half + y_in[step * 3].astype(F32)
    kept[pl.ds(0, tall)] = first_half
    save_first = pltpu.make_async_copy(kept.at[pl.ds(0, tall)], image_out.at[pl.ds(0, tall)], local_sem.at[2])
    save_first.start()
    x_copy(1).wait_recv()
    kept[pl.ds(tall, tall)] += x_in[chunk_rows(1)].astype(F32)
    save_image = pltpu.make_async_copy(kept.at[pl.ds(tall, tall)], image_out.at[pl.ds(tall, tall)], local_sem.at[0])
    save_image.start()
    for step in range(1, lanes):
        for kind in range(3):
            y_copy(lax.rem(y + step, lanes), kind).wait_send()
    x_copy(1).wait_send()

    def settle_grads(q, carry):
        @pl.when(q != p)
        def _():
            def one_part(k, carry):
                grad_copy(q, k, True).wait_send()
                return carry

            lax.fori_loop(0, parts, one_part, 0)

        return carry

    lax.fori_loop(0, planes, settle_grads, 0)

    def settle_chunks(m, carry):
        c_copy(0, m).wait_send()
        c_copy(1, m).wait_send()

        @pl.when(m % 2 == 0)
        def _():
            x_copy(m).wait_send()

        return carry

    lax.fori_loop(0, chunks, settle_chunks, 0)
    for k in range(parts):
        save_text(k).wait()
    save_first.wait()
    save_image.wait()


def solution(mesh):
    lanes = mesh.shape["lane"]
    planes = mesh.shape["block"] // 4
    cuts = 4

    def on_device(images, texts, labels):
        rows, width = images.shape
        share = rows // lanes
        parts = min(8, share // 16)
        pieces = min(8, share // 16)
        chunks = 2 * lanes
        dma = lambda n: pltpu.SemaphoreType.DMA((n,))
        hbm = pl.BlockSpec(memory_space=pltpu.HBM)
        free = pl.BlockSpec(memory_space=pl.ANY)
        half = lambda *s: pltpu.VMEM(s, BF16)
        full = lambda *s: pltpu.VMEM(s, F32)
        return pl.pallas_call(
            functools.partial(kernel, planes, lanes, parts, pieces, cuts),
            out_shape=(
                jax.ShapeDtypeStruct((share, width), F32),
                jax.ShapeDtypeStruct((share, width), F32),
            ),
            in_specs=[hbm, hbm, hbm],
            out_specs=(free, free),
            scratch_shapes=[
                half(4 * rows, width),
                half(planes, share, width),
                pltpu.VMEM((4, 1, rows), jnp.int32),
                full(4 * rows, width),
                full(planes, share, width),
                half(planes, share, width),
                half(planes, share, width),
                half(planes, share, width),
                half(2, rows, width),
                half(2, rows, width),
                half(rows, width),
                half(rows, width),
                half(3 * lanes, share // 2, width),
                half(3 * lanes, share // 2, width),
                full(share, width),
                dma(3), dma(1), dma(1), dma(pieces), *[dma(lanes * pieces)] * 4,
                dma(3), dma(3), *[dma(cuts * planes)] * 3,
                dma(planes * parts), dma(planes * parts), dma(planes * parts),
                dma(2 * chunks), dma(2 * chunks), dma(chunks), dma(chunks), dma(3 * lanes), dma(3 * lanes), dma(parts),
            ],
            compiler_params=pltpu.CompilerParams(
                collective_id=0, has_side_effects=True, vmem_limit_bytes=50 * 1024 * 1024
            ),
        )(images, texts, labels.reshape(1, rows))

    return jax.shard_map(
        on_device,
        mesh=mesh,
        in_specs=(P("block", None), P("block", None), P("block")),
        out_specs=(P(("block", "lane"), None), P(("block", "lane"), None)),
        check_vma=False,
    )
```
